128 devices in a mesh: grain: 32 (over y, z, core), cell: 4 (over x).
Axes of the slice: x: 4, y: 4, z: 4, core: 2. Of those that a mesh axis runs over, the one named last changes fastest.
Arguments:
- displacement: float32 [4096, 3, 768], P(('grain', 'cell')), may hold values from -0.1 to 0.1
- velocity: float32 [4096, 3, 768], P(('grain', 'cell')), may hold values from -6 to 6
- centers: float32 [3, 4096], P(None, ('grain', 'cell')), may hold values from -4 to 4
- tile_list: int32 [4096, 4, 2], P(('grain', 'cell')), may hold values from 0 to 5
- broken_bits: int32 [4096, 4, 2048], P(('grain', 'cell')), may hold values from 0 to 255, as said below
- surface_nodes: int32 [4096, 512], P(('grain', 'cell')), may hold values from 0 to 767, as said below
- send_order: int32 [128, 128], P(('grain', 'cell')), may hold values from 0 to 127, each once within a row
- pair_list: int32 [128, 128, 2], P(('grain', 'cell')), may hold values from 0 to 127
- pair_count: int32 [128], P(('grain', 'cell')), may hold values from 1 to 128, 8192 in all
Outputs:
- force: float32 [4096, 3, 768], P(('grain', 'cell'))
- new_velocity: float32 [4096, 3, 768], P(('grain', 'cell'))
The draws below stay inside these ranges and needn't reach their ends.
Inputs may be any that keep to these rules, and one draw needn't show every extreme that they name: `surface_nodes`: within a grain the 512 surface node indices are distinct. `send_order`: each row is a permutation of the device's 128 surface blocks; position p goes to device p div 1, so every device receives exactly 1 block from each device. `broken_bits`: each word packs 8 broken flags, any bit pattern.
All inputs are finite; a program needn't handle non-finite values. No bound on the sum of `pair_count` on one device may be relied on, other than what follows from the above.
Results may differ from the reference program's by a relative error of at most 0.0003.
Values sent between devices are 32-bit elements; how exact they have to be, the bound alone decides.
No kernel may reach another device: no remote copies, remote signals or barrier semaphores. Data moves between devices by JAX's collectives and lax.ppermute only.
A program may use at most 64 MiB of HBM per device.

```python
import math
import jax
import jax.numpy as jnp
import numpy as np
from jax import lax

NODES = 768
BLK = 128
SB = 4
TILES_G = 4
PAIRS_DEV = 128
OWNERS = 128
GRAINS = 4096
SBLK_DEV = 128
SURF = 512
CAP = 1
WORDS = 2048


def draw_broken_bits(key, part):
    shape_all = (GRAINS, TILES_G, WORDS)
    keys = jax.random.split(jax.random.fold_in(key, 7), 3)
    first_word = jax.random.randint(keys[0], shape_all, 0, 256, dtype=jnp.int32)
    second_word = jax.random.randint(keys[1], shape_all, 0, 256, dtype=jnp.int32)
    third_word = jax.random.randint(keys[2], shape_all, 0, 256, dtype=jnp.int32)
    combined = first_word & second_word & third_word
    return combined.at[0, 0, 0].set(255)


def draw_surface_nodes(key, part):
    keys = jax.random.split(jax.random.fold_in(key, 13), GRAINS)

    def one_grain(grain_key):
        return jax.random.permutation(grain_key, NODES)[:SURF].astype(jnp.int32)
    return jax.vmap(one_grain)(keys)


def touch_ends(values, stream_key, smallest, top_value):
    dims = values.shape
    spot = [jax.random.randint(jax.random.fold_in(stream_key, axis), (), 0, dims[axis]) for axis in range(len(dims))]
    values = values.at[tuple(spot)].set(smallest)
    longest = dims.index(max(dims))
    spot[longest] = (spot[longest] + 1) % dims[longest]
    return values.at[tuple(spot)].set(top_value)


def shard_levels(stream_key, shape, cuts, low, top_value):
    def one(position, blocks):
        draws = jax.random.uniform(jax.random.fold_in(jax.random.fold_in(stream_key, 6), position), (blocks,), jnp.float32, low / len(cuts), top_value / len(cuts))
        return jnp.repeat(jnp.exp(draws), shape[position] // blocks).reshape((-1,) + (1,) * (len(shape) - position - 1))

    loudness = one(*cuts[0])
    for cut in cuts[1:]:
        loudness = loudness * one(*cut)
    return loudness


def length_profile(amount, total, most, slope):
    portions = [(1 << 20) // math.isqrt(grade ** slope) + 1 for grade in range(2, amount + 1)]
    spare, holding = total - most - (amount - 1), [1] * (amount - 1)
    while spare > 0:
        movable = [i for i in range(amount - 1) if holding[i] < most]
        mass, left = sum([portions[i] for i in movable]), spare
        for i in movable:
            extra = min(most - holding[i], max(1, left * portions[i] // mass), spare)
            holding[i] = holding[i] + extra
            spare = spare - extra
    return np.array([most] + holding)


def ragged_sizes(stream_key, count, total, bound, skew):
    if count == 2:
        one = jax.random.randint(stream_key, (), max(1, total - bound), min(bound, total - 1) + 1)
        return jnp.stack([one, total - one])
    lengths = jnp.asarray(length_profile(count, total, bound, skew), jnp.int32)
    pairs = (count - 1) // 2
    source_of, taker = lengths[1:1 + 2 * pairs:2], lengths[2:2 + 2 * pairs:2]
    margin = jnp.minimum(source_of - 1, bound - taker)
    shifted = jax.random.randint(jax.random.fold_in(stream_key, 1), (pairs,), 0, 1 << 20) % (margin + 1)
    lengths = lengths.at[1:1 + 2 * pairs:2].set(source_of - shifted).at[2:2 + 2 * pairs:2].set(taker + shifted)
    return lengths[jax.random.permutation(jax.random.fold_in(stream_key, 2), count)]


def scatter_about(own_key, extent, deviation, reach, pieces=(), kind=jnp.bfloat16):
    drawn = deviation * jax.random.normal(own_key, extent, jnp.float32)
    if pieces:
        drawn = drawn * shard_levels(own_key, extent, pieces, -0.22, 0.18)
    return jnp.clip(drawn, -reach, reach).astype(kind)


def setup_inputs(seed: int = 0) -> dict:
    seeds = jax.random.split(jax.random.key(seed), 10)
    return {
        "displacement": scatter_about(seeds[0], (GRAINS, 3, NODES), 0.02, 0.1, ((0, 128),), jnp.float32),
        "velocity": scatter_about(seeds[1], (GRAINS, 3, NODES), 1.0, 6.0, ((0, 128),), jnp.float32),
        "centers": jnp.clip(jax.random.uniform(seeds[2], (3, GRAINS), jnp.float32, -4.0, 4.0) * shard_levels(seeds[2], (3, GRAINS), ((1, 128),), -0.4, 0.0), -4.0, 4.0),
        "tile_list": touch_ends(jax.random.randint(seeds[3], (GRAINS, TILES_G, 2), 0, NODES // BLK), jax.random.fold_in(seeds[3], 1), 0, (NODES // BLK) - 1).astype(jnp.int32),
        "broken_bits": draw_broken_bits(jax.random.fold_in(seeds[9], 71), 0),
        "surface_nodes": draw_surface_nodes(jax.random.fold_in(seeds[9], 71), 0),
        "send_order": jax.vmap(lambda own: jax.random.permutation(own, SBLK_DEV))(jax.random.split(seeds[6], OWNERS)).reshape((OWNERS, SBLK_DEV)).astype(jnp.int32),
        "pair_list": touch_ends(jax.random.randint(seeds[7], (OWNERS, PAIRS_DEV, 2), 0, SBLK_DEV), jax.random.fold_in(seeds[7], 1), 0, SBLK_DEV - 1).astype(jnp.int32),
        "pair_count": ragged_sizes(seeds[8], OWNERS, OWNERS * PAIRS_DEV // 2, PAIRS_DEV, 2).astype(jnp.int32),
    }


HORIZON = 3.0
BOND_STIFF = 5.0
CONTACT_STIFF = 0.02
CONTACT_DAMP = 0.05
CONTACT_RANGE = 9.0
TIME_STEP = 0.5

def lattice(node_count):
    node_index = jnp.arange(node_count, dtype=jnp.int32)
    return jnp.stack([node_index % 8, node_index // 8 % 8, node_index // 64]).astype(jnp.float32)

def unpack(bit_words):
    shifts = jnp.arange(8, dtype=jnp.int32)
    bit_table = jnp.right_shift(bit_words[:, None], shifts[None, :]) & 1
    return bit_table.reshape(BLK, BLK)

def bond_tile(rest_grid, now_grid, tile_pair, tile_words):
    row_start = tile_pair[0] * BLK
    col_start = tile_pair[1] * BLK
    rest_rows = lax.dynamic_slice_in_dim(rest_grid, row_start, BLK, 1)
    rest_cols = lax.dynamic_slice_in_dim(rest_grid, col_start, BLK, 1)
    now_rows = lax.dynamic_slice_in_dim(now_grid, row_start, BLK, 1)
    now_cols = lax.dynamic_slice_in_dim(now_grid, col_start, BLK, 1)
    rest_gap = rest_cols[:, None, :] - rest_rows[:, :, None]
    rest_len = jnp.sqrt(lax.optimization_barrier(jnp.sum(rest_gap * rest_gap, axis=0)))
    now_gap = now_cols[:, None, :] - now_rows[:, :, None]
    now_len = jnp.sqrt(lax.optimization_barrier(jnp.sum(now_gap * now_gap, axis=0)))
    live_bond = (rest_len > 0.5) & (rest_len <= HORIZON) & (unpack(tile_words) == 0)
    safe_rest = jnp.where(live_bond, rest_len, 1.0)
    safe_now = jnp.where(live_bond, now_len, 1.0)
    coefficient = jnp.where(live_bond, BOND_STIFF * (now_len - rest_len) / (safe_rest * safe_now), 0.0)
    return lax.optimization_barrier(jnp.sum(coefficient[None] * now_gap, axis=2))

def grain_bonds(displacement, tile_list, bit_words):
    rest_grid = lattice(displacement.shape[1])
    now_grid = rest_grid + displacement

    def tile_step(force_sum, entry_item):
        tile_pair, tile_words = entry_item
        tile_force = bond_tile(rest_grid, now_grid, tile_pair, tile_words)
        row_start = tile_pair[0] * BLK
        old_rows = lax.dynamic_slice_in_dim(force_sum, row_start, BLK, 1)
        return (lax.dynamic_update_slice_in_dim(force_sum, old_rows + tile_force, row_start, 1), None)
    force_sum, _ = lax.scan(tile_step, jnp.zeros_like(displacement), (tile_list, bit_words))
    return force_sum

def bonds_all(displacement, tile_list, bit_words):
    grains = displacement.shape[0]

    def grouped(array):
        return array.reshape((grains // 16, 16) + array.shape[1:])

    def group_step(entry_item):
        return jax.vmap(grain_bonds)(*entry_item)
    forces = lax.map(group_step, (grouped(displacement), grouped(tile_list), grouped(bit_words)))
    return forces.reshape(displacement.shape)

def contact_pair(left_block, right_block):
    gap_vec = left_block[:3, :, None] - right_block[:3, None, :]
    slip_vec = left_block[3:, :, None] - right_block[3:, None, :]
    weights = jnp.exp(-lax.optimization_barrier(jnp.sum(gap_vec * gap_vec, axis=0)) / CONTACT_RANGE)
    push_term = weights[None] * (CONTACT_STIFF * gap_vec - CONTACT_DAMP * slip_vec)
    return (lax.optimization_barrier(jnp.sum(push_term, axis=2)), -lax.optimization_barrier(jnp.sum(push_term, axis=1)))

def surface_blocks(displacement, velocity, centers, surface_nodes):
    rest_grid = lattice(displacement.shape[2])
    now_grid = rest_grid[None] + displacement + centers.T[:, :, None]
    full_state = jnp.concatenate([now_grid, velocity], axis=1)
    picked = jnp.take_along_axis(full_state, surface_nodes[:, None, :], axis=2)
    grains = picked.shape[0]
    return picked.reshape(grains, 6, SB, BLK).transpose(0, 2, 1, 3).reshape(grains * SB, 6, BLK)

def spread_surface(block_force, surface_nodes, node_count):
    grains = surface_nodes.shape[0]
    surface_force = block_force.reshape(grains, SB, 3, BLK).transpose(0, 2, 1, 3).reshape(grains, 3, SB * BLK)

    def one_grain(node_ids, node_force):
        return jnp.zeros((3, node_count), node_force.dtype).at[:, node_ids].add(node_force)
    return jax.vmap(one_grain)(surface_nodes, surface_force)

def reference(displacement, velocity, centers, tile_list, broken_bits, surface_nodes, send_order, pair_list, pair_count):
    bond_force = bonds_all(displacement, tile_list, broken_bits)
    blocks = surface_blocks(displacement, velocity, centers, surface_nodes)
    anchor = jnp.arange(OWNERS, dtype=jnp.int32)[:, None, None] * SBLK_DEV
    held_ids = (send_order.reshape(OWNERS, OWNERS, CAP) + anchor).transpose(1, 0, 2).reshape(OWNERS, SBLK_DEV)
    left_ids = jnp.take_along_axis(held_ids, pair_list[:, :, 0], axis=1)
    right_ids = jnp.take_along_axis(held_ids, pair_list[:, :, 1], axis=1)
    live_pairs = jnp.arange(PAIRS_DEV, dtype=jnp.int32)[None, :] < pair_count[:, None]

    def owner_step(accumulated, entry_item):
        left_one, right_one, in_range = entry_item
        left_force, right_force = jax.vmap(contact_pair)(blocks[left_one], blocks[right_one])
        live_mask = in_range.astype(left_force.dtype)[:, None, None]
        accumulated = accumulated.at[left_one].add(left_force * live_mask)
        accumulated = accumulated.at[right_one].add(right_force * live_mask)
        return (accumulated, None)
    start_force = jnp.zeros((blocks.shape[0], 3, BLK), blocks.dtype)
    block_force, _ = lax.scan(owner_step, start_force, (left_ids, right_ids, live_pairs))
    contact_force = spread_surface(block_force, surface_nodes, displacement.shape[2])
    force = bond_force + contact_force
    return (force, velocity + TIME_STEP * force)
```

```python
import functools
import math

import jax
import jax.numpy as jnp
from jax import lax
from jax.experimental import pallas as pl
from jax.experimental.pallas import tpu as pltpu
from jax.sharding import PartitionSpec as P

BLK = 128
SB = 4
GRAINS_DEV = 32
NODES = 768
NB = NODES // BLK
SLOTS = 128
GROUPS = GRAINS_DEV // 8

CONTACT_STIFF = 0.02
CONTACT_DAMP = 0.05
CONTACT_RANGE = 9.0
TIME_STEP = 0.5
BOND_STIFF = 5.0
HORIZON = 3.0
ORIGIN = (3.5, 3.5, 5.5)
LANE = 1
F32 = jnp.float32
BF16 = jnp.bfloat16
VMEM_LIMIT = 60000 * 1024


def pieces(value, count):
    parts = []
    rest = value
    for step in range(count):
        head = rest.astype(BF16).astype(F32)
        parts.append(head)
        if step + 1 < count:
            rest = rest - head
    return parts


def lane_gather(source, index):
    return jnp.take_along_axis(source, index, axis=1, mode="promise_in_bounds")


def lane_iota(shape):
    return lax.broadcasted_iota(jnp.int32, shape, len(shape) - 1)


def sublane_iota(shape):
    return lax.broadcasted_iota(jnp.int32, shape, 0)


def gather_kernel(send_ref, disp_ref, vel_ref, centers_ref, nodes_ref, out_ref, state_ref):
    for group in range(GROUPS):
        grains = pl.ds(8 * group, 8)
        own = lane_iota((8, GRAINS_DEV)) == sublane_iota((8, GRAINS_DEV)) + 8 * group
        offsets = [
            jnp.sum(
                jnp.where(own, jnp.broadcast_to(centers_ref[c : c + 1, :], own.shape), 0.0),
                axis=1,
                keepdims=True,
            )
            for c in range(3)
        ]
        for k in range(SB):
            node = nodes_ref[grains, k * BLK : (k + 1) * BLK]
            lane = node & (BLK - 1)
            block = node >> 7
            rest = (node & 7, (node >> 3) & 7, node >> 6)
            for c in range(6):
                ref = disp_ref if c < 3 else vel_ref
                value = jnp.zeros((8, BLK), F32)
                for a in range(NB):
                    source = ref[grains, c % 3, a * BLK : (a + 1) * BLK]
                    value = jnp.where(block == a, lane_gather(source, lane), value)
                if c < 3:
                    value = rest[c].astype(F32) + value + offsets[c]
                state_ref[pl.ds(group * 256 + k * 8 + c, 8, stride=32), :] = value
    for d in range(SLOTS):
        row = pl.multiple_of(send_ref[0, d] * 8, 8)
        out_ref[6 * d : 6 * d + 6, :] = state_ref[pl.ds(row, 8), :][:6]


def surface_blocks(send_order, displacement, velocity, centers, surface_nodes):
    vmem = pl.BlockSpec(memory_space=pltpu.VMEM)
    return pl.pallas_call(
        gather_kernel,
        out_shape=jax.ShapeDtypeStruct((SLOTS * 6, BLK), F32),
        in_specs=[pl.BlockSpec(memory_space=pltpu.SMEM), vmem, vmem, vmem, vmem],
        out_specs=vmem,
        scratch_shapes=[pltpu.VMEM((SLOTS * 8, BLK), F32)],
        name="surface_blocks",
    )(send_order, displacement, velocity, centers, surface_nodes)


PAIR_UNROLL = 4


def contact_kernel(count_ref, pairs_ref, state_ref, out_ref, left_ref, right_ref, slide_ref, acc_ref):
    scale = math.log2(math.e) / CONTACT_RANGE
    one = jnp.ones((8, BLK), F32)
    zero = jnp.zeros((8, BLK), F32)

    def put(ref, rows, first, slot, values):
        for n, value in enumerate(values):
            ref[pl.ds(slot * rows + first + n, 8, stride=rows), :] = value

    def prepare(group, carry):
        first = group * 48
        place = [state_ref[pl.ds(first + c, 8, stride=6), :] - ORIGIN[c] for c in range(3)]
        speed = [state_ref[pl.ds(first + 3 + c, 8, stride=6), :] for c in range(3)]
        slot = group * 8
        norm = place[0] * place[0] + place[1] * place[1] + place[2] * place[2]
        norm = pieces(-scale * norm, 3)
        left, right, slide = [], [], []
        for c in range(3):
            p1, p2, p3 = pieces(place[c], 3)
            q1, q2, q3 = pieces(place[c] * (2.0 * scale), 3)
            left += [p1, p1, p2, p2, p1, p3]
            right += [q1, q2, q1, q2, q3, q1]
        left += norm + [one] * 3 + [zero] * 8
        right += [one] * 3 + norm + [zero] * 8
        for c in range(3):
            slide += pieces(CONTACT_STIFF * place[c] - CONTACT_DAMP * speed[c], 3)
        slide += [one] + [zero] * 6
        put(left_ref, 32, 0, slot, left)
        put(right_ref, 32, 0, slot, right)
        put(slide_ref, 16, 0, slot, slide)
        return carry

    lax.fori_loop(0, SLOTS // 8, prepare, 0)
    acc_ref[...] = jnp.zeros_like(acc_ref)
    total = count_ref[0]

    def batch(step, carry):
        live = []
        for n in range(PAIR_UNROLL):
            flat = step * PAIR_UNROLL + n
            in_range = flat < total
            at = jnp.minimum(flat, SLOTS - 1)
            i = jnp.where(in_range, pairs_ref[0, at, 0], 0)
            j = jnp.where(in_range, pairs_ref[0, at, 1], 0)
            left = left_ref[pl.ds(pl.multiple_of(i * 32, 32), 32), :]
            right = right_ref[pl.ds(pl.multiple_of(j * 32, 32), 32), :].astype(BF16)
            exponent = jnp.dot(left.T.astype(BF16), right, preferred_element_type=F32)
            weight = jnp.exp2(exponent)
            high = weight.astype(BF16)
            low = (weight - high.astype(F32)).astype(BF16)
            slide_i = slide_ref[pl.ds(pl.multiple_of(i * 16, 16), 16), :].astype(BF16)
            slide_j = slide_ref[pl.ds(pl.multiple_of(j * 16, 16), 16), :].astype(BF16)
            across = (((1,), (1,)), ((), ()))
            down = (((1,), (0,)), ((), ()))
            to_i = lax.dot_general(slide_j, high, across, preferred_element_type=F32)
            to_i += lax.dot_general(slide_j, low, across, preferred_element_type=F32)
            to_j = lax.dot_general(slide_i, high, down, preferred_element_type=F32)
            to_j += lax.dot_general(slide_i, low, down, preferred_element_type=F32)
            live.append((jnp.where(in_range, i, SLOTS), jnp.where(in_range, j, SLOTS), to_i, to_j))
        for i, j, to_i, to_j in live:
            rows_i = pl.ds(pl.multiple_of(i * 16, 16), 16)
            acc_ref[rows_i, :] += to_i
            rows_j = pl.ds(pl.multiple_of(j * 16, 16), 16)
            acc_ref[rows_j, :] += to_j
        return carry

    lax.fori_loop(0, (total + PAIR_UNROLL - 1) // PAIR_UNROLL, batch, 0)

    def finish(group, carry):
        slot = group * 8

        def row(ref, n):
            return ref[pl.ds(slot * 16 + n, 8, stride=16), :]

        total_weight = row(acc_ref, 9)
        for c in range(3):
            own = row(slide_ref, 3 * c) + row(slide_ref, 3 * c + 1) + row(slide_ref, 3 * c + 2)
            other = row(acc_ref, 3 * c) + row(acc_ref, 3 * c + 1) + row(acc_ref, 3 * c + 2)
            out_ref[pl.ds(slot * 3 + c, 8, stride=3), :] = own * total_weight - other
        return carry

    lax.fori_loop(0, SLOTS // 8, finish, 0)


def contact_forces(pair_count, pair_list, state):
    vmem = pl.BlockSpec(memory_space=pltpu.VMEM)
    smem = pl.BlockSpec(memory_space=pltpu.SMEM)
    return pl.pallas_call(
        contact_kernel,
        out_shape=jax.ShapeDtypeStruct((SLOTS * 3, BLK), F32),
        in_specs=[smem, smem, vmem],
        out_specs=vmem,
        scratch_shapes=[
            pltpu.VMEM((SLOTS * 32, BLK), F32),
            pltpu.VMEM((SLOTS * 32, BLK), F32),
            pltpu.VMEM((SLOTS * 16, BLK), F32),
            pltpu.VMEM(((SLOTS + 1) * 16, BLK), F32),
        ],
        name="contact_forces",
    )(pair_count, pair_list, state)


def bond_kernel(
    tiles_ref, disp_ref, words_ref, nodes_ref, out_ref, inverse_ref, base_ref, cross_ref, square_ref, acc_ref
):
    lane = lane_iota((8, BLK))

    def lattice(a, c):
        index = lane + a * BLK
        return ((index & 7, (index >> 3) & 7, index >> 6)[c]).astype(F32) - ORIGIN[c]

    one = jnp.ones((8, BLK), F32)
    zero = jnp.zeros((8, BLK), F32)
    sub = sublane_iota((8, BLK))
    fixed = []
    for a in range(NB):
        rows = jnp.where(sub < 6, 0.0, 1.0)
        for c in range(3):
            rows = jnp.where((sub == c) | (sub == c + 3), -2.0 * lattice(a, c), rows)
        fixed.append(rows)
        base_ref[GRAINS_DEV * NB * 8 + a * 8 : GRAINS_DEV * NB * 8 + a * 8 + 8, :] = rows

    for group in range(GROUPS):
        grains = pl.ds(8 * group, 8)
        for a in range(NB):
            high, low, growth = [], [], None
            for c in range(3):
                shift = disp_ref[grains, c, a * BLK : (a + 1) * BLK]
                u1, u2 = pieces(shift, 2)
                high.append(u1)
                low.append(u2)
                both = u1 + u2
                term = both * (2.0 * lattice(a, c) + both)
                growth = term if growth is None else growth + term
            g1, g2, g3 = pieces(growth, 3)
            row = (group * 8 * NB + a) * 8
            for n, value in enumerate(high + low + [g1, g2]):
                base_ref[pl.ds(row + n, 8, stride=NB * 8), :] = value
            for n, value in enumerate(high + low + [g3, one]):
                cross_ref[pl.ds(row + n, 8, stride=NB * 8), :] = value
            minus_high = [-2.0 * v for v in high]
            minus_low = [-2.0 * v for v in low]
            row = (group * 8 * NB + a) * 16
            for n, value in enumerate(
                minus_high + minus_low + [one, g3] + minus_low + minus_high + [zero, zero]
            ):
                square_ref[pl.ds(row + n, 8, stride=NB * 16), :] = value

    acc_ref[...] = jnp.zeros_like(acc_ref)

    sub128 = sublane_iota((BLK, SB * BLK))
    sub16 = sublane_iota((16, SB * BLK))
    k_index = lane_iota((16, SB * BLK))
    k_value = jnp.where(sub16 < 8, k_index & 127, 1 + (k_index >> 7)).astype(F32)

    tile_row = sublane_iota((BLK, BLK))
    tile_col = lane_iota((BLK, BLK))
    spread = jnp.where((tile_row & 15) == (tile_col >> 3), 1.0, 0.0).astype(BF16)
    own_lane = (lane >> 4) == sub
    dx = (tile_row & 7) - (tile_col & 7)
    dy = ((tile_row >> 3) & 7) - ((tile_col >> 3) & 7)
    flat_square = dx * dx + dy * dy
    flag = jnp.left_shift(jnp.ones((BLK, BLK), jnp.int32), tile_col & 7)

    def grain_step(grain, carry):
        node = nodes_ref[pl.ds(grain, 1), :]
        hit = jnp.where(jnp.broadcast_to(node & 127, (BLK, SB * BLK)) == sub128, 1.0, 0.0).astype(BF16)
        value = jnp.where(jnp.broadcast_to(node >> 7, (16, SB * BLK)) == (sub16 & 7), k_value, 0.0).astype(BF16)
        inverse_ref[pl.ds(pl.multiple_of(grain * 16, 16), 16), :] = lax.dot_general(
            value, hit, (((1,), (1,)), ((), ())), preferred_element_type=F32
        )
        found = []
        for t in range(4):
            a = tiles_ref[grain, t, 0]
            b = tiles_ref[grain, t, 1]
            row_a = pl.multiple_of((grain * NB + a) * 8, 8)
            row_b = pl.multiple_of((grain * NB + b) * 8, 8)
            fixed_a = base_ref[pl.ds(pl.multiple_of((GRAINS_DEV * NB + a) * 8, 8), 8), :]
            fixed_b = base_ref[pl.ds(pl.multiple_of((GRAINS_DEV * NB + b) * 8, 8), 8), :]
            base_a = base_ref[pl.ds(row_a, 8), :]
            base_b = base_ref[pl.ds(row_b, 8), :]
            left = jnp.concatenate([base_a, fixed_a, cross_ref[pl.ds(row_a, 8), :], base_a], axis=0)
            right = jnp.concatenate(
                [fixed_b, base_b, square_ref[pl.ds(pl.multiple_of((grain * NB + b) * 16, 16), 16), :]],
                axis=0,
            ).astype(BF16)
            growth = jnp.dot(left.T.astype(BF16), right, preferred_element_type=F32)
            words = words_ref[pl.ds(grain * 64 + t, 16, stride=4), :].astype(F32)
            picked = jnp.concatenate(
                [jnp.where(own_lane, jnp.broadcast_to(words[r : r + 1, :], (8, BLK)), 0.0) for r in range(16)],
                axis=0,
            ).astype(BF16)
            word = jnp.dot(picked, spread, preferred_element_type=F32).astype(jnp.int32)
            dz = (tile_row >> 6) - (tile_col >> 6) + 2 * (a - b)
            rest_square = flat_square + dz * dz
            live = (rest_square >= 1) & (rest_square <= 9) & ((word & flag) == 0)
            rest = rest_square.astype(F32)
            pull = jnp.where(live, lax.rsqrt(jnp.maximum(rest, 1.0)) - lax.rsqrt(rest + growth), 0.0)
            high = pull.astype(BF16)
            low = (pull - high.astype(F32)).astype(BF16)
            moments = jnp.concatenate([base_b, fixed_b], axis=0).astype(BF16)
            across = (((1,), (1,)), ((), ()))
            force = lax.dot_general(moments, high, across, preferred_element_type=F32)
            force += lax.dot_general(moments, low, across, preferred_element_type=F32)
            found.append((pl.multiple_of((grain * NB + a) * 16, 16), force))
        for row, force in found:
            acc_ref[pl.ds(row, 16), :] += force
        return carry

    lax.fori_loop(0, GRAINS_DEV, grain_step, 0)

    for group in range(GROUPS):
        for a in range(NB):
            row = (group * 8 * NB + a) * 16
            acc = [acc_ref[pl.ds(row + n, 8, stride=NB * 16), :] for n in range(15)]
            base = (group * 8 * NB + a) * 8
            for c in range(3):
                own = lattice(a, c) + (
                    base_ref[pl.ds(base + c, 8, stride=NB * 8), :]
                    + base_ref[pl.ds(base + 3 + c, 8, stride=NB * 8), :]
                )
                force = acc[c] + acc[3 + c] - 0.5 * acc[8 + c] - acc[14] * own
                out_ref[pl.ds(8 * group, 8), c, a * BLK : (a + 1) * BLK] = force * BOND_STIFF


def bond_forces(tile_list, displacement, words, surface_nodes):
    vmem = pl.BlockSpec(memory_space=pltpu.VMEM)
    smem = pl.BlockSpec(memory_space=pltpu.SMEM)
    rows = GRAINS_DEV * NB
    return pl.pallas_call(
        bond_kernel,
        out_shape=(
            jax.ShapeDtypeStruct((GRAINS_DEV, 3, NODES), F32),
            jax.ShapeDtypeStruct((GRAINS_DEV * 16, BLK), F32),
        ),
        in_specs=[smem, vmem, vmem, vmem],
        out_specs=(vmem, vmem),
        scratch_shapes=[
            pltpu.VMEM(((rows + NB) * 8, BLK), F32),
            pltpu.VMEM((rows * 8, BLK), F32),
            pltpu.VMEM((rows * 16, BLK), F32),
            pltpu.VMEM((rows * 16, BLK), F32),
        ],
        cost_estimate=pl.CostEstimate(flops=4_000_000_000, transcendentals=2_000_000, bytes_accessed=2_000_000),
        name="bond_forces",
    )(tile_list, displacement, words, surface_nodes)


def sum_kernel(send_ref, back_ref, inverse_ref, bond_ref, vel_ref, force_ref, new_ref, block_ref):
    for d in range(SLOTS):
        row = pl.multiple_of(send_ref[0, d] * 8, 8)
        block_ref[pl.ds(row, 3), :] = back_ref[3 * d : 3 * d + 3, :]
    for group in range(GROUPS):
        grains = pl.ds(8 * group, 8)
        for a in range(NB):
            lane = inverse_ref[pl.ds(group * 128 + a, 8, stride=16), :].astype(jnp.int32)
            block = inverse_ref[pl.ds(group * 128 + 8 + a, 8, stride=16), :].astype(jnp.int32)
            columns = slice(a * BLK, (a + 1) * BLK)
            for c in range(3):
                value = jnp.zeros((8, BLK), F32)
                for k in range(SB):
                    source = block_ref[pl.ds(group * 256 + k * 8 + c, 8, stride=32), :]
                    value = jnp.where(block == k + 1, lane_gather(source, lane), value)
                force = bond_ref[grains, c, columns] + value
                force_ref[grains, c, columns] = force
                new_ref[grains, c, columns] = vel_ref[grains, c, columns] + TIME_STEP * force


def sum_forces(send_order, returned, inverse, bond, velocity):
    vmem = pl.BlockSpec(memory_space=pltpu.VMEM)
    shape = jax.ShapeDtypeStruct((GRAINS_DEV, 3, NODES), F32)
    return pl.pallas_call(
        sum_kernel,
        out_shape=(shape, shape),
        in_specs=[pl.BlockSpec(memory_space=pltpu.SMEM), vmem, vmem, vmem, vmem],
        out_specs=(vmem, vmem),
        scratch_shapes=[pltpu.VMEM((SLOTS * 8, BLK), F32)],
        name="sum_forces",
    )(send_order, returned, inverse, bond, velocity)


def exchange(rows, width):
    moved = lax.all_to_all(
        rows.reshape(SLOTS, 1, width, BLK), ("grain", "cell"), split_axis=0, concat_axis=0, tiled=True
    )
    return moved.reshape(SLOTS * width, BLK)


def on_device(
    displacement,
    velocity,
    centers,
    tile_list,
    broken_bits,
    surface_nodes,
    send_order,
    pair_list,
    pair_count,
):
    words = broken_bits.reshape(GRAINS_DEV, 4, 16, BLK).transpose(0, 2, 1, 3).reshape(GRAINS_DEV * 64, BLK)
    outgoing = surface_blocks(send_order, displacement, velocity, centers, surface_nodes)
    received = exchange(outgoing, 6)
    bond, inverse = bond_forces(tile_list, displacement, words, surface_nodes)
    slot_force = contact_forces(pair_count, pair_list, received)
    returned = exchange(slot_force, 3)
    return sum_forces(send_order, returned, inverse, bond, velocity)


def solution(mesh):
    return jax.shard_map(
        on_device,
        mesh=mesh,
        in_specs=(
            P(("grain", "cell"), None, None),
            P(("grain", "cell"), None, None),
            P(None, ("grain", "cell")),
            P(("grain", "cell"), None, None),
            P(("grain", "cell"), None, None),
            P(("grain", "cell"), None),
            P(("grain", "cell"), None),
            P(("grain", "cell"), None, None),
            P(("grain", "cell")),
        ),
        out_specs=(P(("grain", "cell"), None, None), P(("grain", "cell"), None, None)),
        check_vma=False,
    )
```

```python
import functools
import math

import jax
import jax.numpy as jnp
from jax import lax
from jax.experimental import pallas as pl
from jax.experimental.pallas import tpu as pltpu
from jax.sharding import PartitionSpec as P

BLK = 128
SB = 4
GRAINS_DEV = 32
NODES = 768
NB = NODES // BLK
SLOTS = 128
GROUPS = GRAINS_DEV // 8

CONTACT_STIFF = 0.02
CONTACT_DAMP = 0.05
CONTACT_RANGE = 9.0
TIME_STEP = 0.5
BOND_STIFF = 5.0
HORIZON = 3.0
ORIGIN = (3.5, 3.5, 5.5)
LANE = 1
F32 = jnp.float32
BF16 = jnp.bfloat16
MIB = 1 << 20
REACH = 2
ACROSS = (((1,), (1,)), ((), ()))
DOWN = (((1,), (0,)), ((), ()))


def pieces(value, count):
    parts = []
    rest = value
    for step in range(count):
        head = rest.astype(BF16).astype(F32)
        parts.append(head)
        if step + 1 < count:
            rest = rest - head
    return parts


def halves(value):
    high = value.astype(BF16)
    return high, (value - high.astype(F32)).astype(BF16)


def lane_gather(source, index):
    return jnp.take_along_axis(source, index, axis=1, mode="promise_in_bounds")


def lane_iota(shape):
    return lax.broadcasted_iota(jnp.int32, shape, len(shape) - 1)


def sublane_iota(shape):
    return lax.broadcasted_iota(jnp.int32, shape, 0)


def gather_kernel(send_ref, disp_ref, vel_ref, centers_ref, nodes_ref, out_ref, state_ref):
    for group in range(GROUPS):
        grains = pl.ds(8 * group, 8)
        own = lane_iota((8, GRAINS_DEV)) == sublane_iota((8, GRAINS_DEV)) + 8 * group
        offsets = [
            jnp.sum(
                jnp.where(own, jnp.broadcast_to(centers_ref[c : c + 1, :], own.shape), 0.0),
                axis=1,
                keepdims=True,
            )
            for c in range(3)
        ]
        for k in range(SB):
            node = nodes_ref[grains, k * BLK : (k + 1) * BLK]
            lane = node & (BLK - 1)
            block = node >> 7
            rest = (node & 7, (node >> 3) & 7, node >> 6)
            for c in range(6):
                ref = disp_ref if c < 3 else vel_ref
                value = lane_gather(ref[c % 3, grains, :BLK], lane)
                for a in range(1, NB):
                    source = ref[c % 3, grains, a * BLK : (a + 1) * BLK]
                    value = jnp.where(block == a, lane_gather(source, lane), value)
                if c < 3:
                    value = rest[c].astype(F32) + value + offsets[c]
                state_ref[pl.ds((group * SB + k) * 48 + c * 8, 8), :] = value
    for d in range(SLOTS):
        block = send_ref[0, d]
        grain = block >> 2
        row = ((grain >> 3) * SB + (block & 3)) * 48 + (grain & 7)
        out_ref[6 * d : 6 * d + 6, :] = state_ref[pl.ds(row, 6, stride=8), :]


def surface_blocks(send_order, displacement, velocity, centers, surface_nodes):
    vmem = pl.BlockSpec(memory_space=pltpu.VMEM)
    return pl.pallas_call(
        gather_kernel,
        out_shape=jax.ShapeDtypeStruct((SLOTS * 6, BLK), F32),
        in_specs=[pl.BlockSpec(memory_space=pltpu.SMEM), vmem, vmem, vmem, vmem],
        out_specs=vmem,
        scratch_shapes=[pltpu.VMEM((SLOTS * 6, BLK), F32)],
        compiler_params=pltpu.CompilerParams(vmem_limit_bytes=8 * MIB),
        name="surface_blocks",
    )(send_order, displacement, velocity, centers, surface_nodes)


PAIR_UNROLL = 16


def contact_kernel(count_ref, pairs_ref, state_ref, out_ref, left_ref, right_ref, slide_ref, acc_ref):
    scale = math.log2(math.e) / CONTACT_RANGE
    one = jnp.ones((8, BLK), F32)
    pad = jnp.zeros((8, BLK), F32)

    def put(ref, rows, group, values):
        for n, value in enumerate(values):
            ref[pl.ds(pl.multiple_of(group * (rows * 8) + n * 8, 8), 8), :] = value

    def prepare(group, carry):
        first = group * 48
        place = [state_ref[pl.ds(first + c, 8, stride=6), :] - ORIGIN[c] for c in range(3)]
        speed = [state_ref[pl.ds(first + 3 + c, 8, stride=6), :] for c in range(3)]
        norm = place[0] * place[0] + place[1] * place[1] + place[2] * place[2]
        norm = pieces(-scale * norm, 3)
        left, right, slide = [], [], []
        for c in range(3):
            p1, p2, p3 = pieces(place[c], 3)
            q1, q2, q3 = pieces(place[c] * (2.0 * scale), 3)
            left += [p1, p1, p2, p2, p1, p3]
            right += [q1, q2, q1, q2, q3, q1]
        left += norm + [one] * 3
        right += [one] * 3 + norm
        for c in range(3):
            slide += pieces(CONTACT_STIFF * place[c] - CONTACT_DAMP * speed[c], 3)
        slide += [one] + [pad] * 6
        put(left_ref, 24, group, left)
        put(right_ref, 24, group, right)
        put(slide_ref, 16, group, slide)
        return carry

    lax.fori_loop(0, SLOTS // 8, prepare, 0)
    acc_ref[...] = jnp.zeros_like(acc_ref)
    total = count_ref[0]

    def rows(ref, count, slot):
        return ref[pl.ds((slot >> 3) * (count * 8) + (slot & 7), count, stride=8), :]

    def batch(step, carry):
        chosen = []
        for n in range(PAIR_UNROLL):
            flat = step * PAIR_UNROLL + n
            in_range = flat < total
            at = jnp.minimum(flat, SLOTS - 1)
            i = jnp.where(in_range, pairs_ref[0, at], 0)
            j = jnp.where(in_range, pairs_ref[1, at], 0)
            chosen.append((i, j, jnp.where(in_range, i, SLOTS), jnp.where(in_range, j, SLOTS)))
        weights = []
        for i, j, _, _ in chosen:
            left = jnp.concatenate([rows(left_ref, 24, i), pad], axis=0)
            right = jnp.concatenate([rows(right_ref, 24, j), pad], axis=0).astype(BF16)
            exponent = jnp.dot(left.T.astype(BF16), right, preferred_element_type=F32)
            weights.append(jnp.exp2(exponent))
        sums = []
        for (i, j, _, _), weight in zip(chosen, weights):
            slide_i = rows(slide_ref, 16, i).astype(BF16)
            slide_j = rows(slide_ref, 16, j).astype(BF16)
            high, low = halves(weight)
            to_i = lax.dot_general(
                jnp.concatenate([high, low], axis=1),
                jnp.concatenate([slide_j, slide_j], axis=1),
                ACROSS,
                preferred_element_type=F32,
            ).T
            to_j = lax.dot_general(
                jnp.concatenate([slide_i, slide_i], axis=1),
                jnp.concatenate([high, low], axis=0),
                DOWN,
                preferred_element_type=F32,
            )
            sums.append((to_i, to_j))
        for (_, _, i, j), (to_i, to_j) in zip(chosen, sums):
            rows_i = pl.ds(pl.multiple_of(i * 16, 16), 16)
            acc_ref[rows_i, :] += to_i
            rows_j = pl.ds(pl.multiple_of(j * 16, 16), 16)
            acc_ref[rows_j, :] += to_j
        return carry

    lax.fori_loop(0, (total + PAIR_UNROLL - 1) // PAIR_UNROLL, batch, 0)

    def finish(group, carry):
        def acc(n):
            return acc_ref[pl.ds(group * 128 + n, 8, stride=16), :]

        def slide(n):
            return slide_ref[pl.ds(pl.multiple_of(group * 128 + n * 8, 8), 8), :]

        total_weight = acc(9)
        for c in range(3):
            own = slide(3 * c) + slide(3 * c + 1) + slide(3 * c + 2)
            other = acc(3 * c) + acc(3 * c + 1) + acc(3 * c + 2)
            out_ref[pl.ds(group * 24 + c, 8, stride=3), :] = own * total_weight - other
        return carry

    lax.fori_loop(0, SLOTS // 8, finish, 0)


def contact_forces(pair_count, pair_list, state):
    vmem = pl.BlockSpec(memory_space=pltpu.VMEM)
    smem = pl.BlockSpec(memory_space=pltpu.SMEM)
    return pl.pallas_call(
        contact_kernel,
        out_shape=jax.ShapeDtypeStruct((SLOTS * 3, BLK), F32),
        in_specs=[smem, smem, vmem],
        out_specs=vmem,
        scratch_shapes=[
            pltpu.VMEM((SLOTS * 24, BLK), F32),
            pltpu.VMEM((SLOTS * 24, BLK), F32),
            pltpu.VMEM((SLOTS * 16, BLK), F32),
            pltpu.VMEM(((SLOTS + 1) * 16, BLK), F32),
        ],
        compiler_params=pltpu.CompilerParams(vmem_limit_bytes=24 * MIB),
        name="contact_forces",
    )(pair_count, pair_list, state)


TILE_UNROLL = 16
TILES = 4


def bond_kernel(
    first_grain,
    grains,
    tiles_ref,
    disp_ref,
    words_ref,
    out_ref,
    base_ref,
    other_ref,
    fixed_ref,
    rest_ref,
    inverse_rest_ref,
    flag_ref,
    dead_ref,
    acc_ref,
    list_ref,
):
    lane = lane_iota((8, BLK))
    sub = sublane_iota((8, BLK))
    one = jnp.ones((8, BLK), F32)
    zero = jnp.zeros((8, BLK), F32)

    def lattice(a, c):
        index = lane + a * BLK
        return ((index & 7, (index >> 3) & 7, index >> 6)[c]).astype(F32) - ORIGIN[c]

    count = jnp.int32(0)
    for grain in range(grains):
        for t in range(TILES):
            apart = tiles_ref[t, 0, first_grain + grain] - tiles_ref[t, 1, first_grain + grain]
            list_ref[count] = grain * TILES + t
            count += jnp.where((apart >= -REACH) & (apart <= REACH), 1, 0)

    for a in range(NB):
        rows = jnp.where(sub < 6, 0.0, 1.0)
        for c in range(3):
            rows = jnp.where((sub == c) | (sub == c + 3), -2.0 * lattice(a, c), rows)
        fixed_ref[a * 8 : a * 8 + 8, :] = rows

    col_y = (lane >> 3) & 7
    for apart in range(-REACH, REACH + 1):
        for r in range(16):
            dx = sub - (lane & 7)
            dy = (r & 7) - col_y
            dz = (r >> 3) - (lane >> 6) - 2 * apart
            square = dx * dx + dy * dy + dz * dz
            near = (square >= 1) & (square <= 9)
            row = ((apart + REACH) * 16 + r) * 8
            rest = square.astype(F32)
            rest_ref[row : row + 8, :] = rest
            inverse_rest_ref[row : row + 8, :] = lax.rsqrt(jnp.maximum(rest, 1.0))
            flag_ref[row : row + 8, :] = jnp.where(near, jnp.left_shift(1, lane & 7), 0)
            dead_ref[row : row + 8, :] = jnp.where(near, 0, 1)

    for group in range(grains // 8):
        these = pl.ds(first_grain + 8 * group, 8)
        for a in range(NB):
            high, low, growth = [], [], None
            for c in range(3):
                u1, u2 = pieces(disp_ref[c, these, a * BLK : (a + 1) * BLK], 2)
                high.append(u1)
                low.append(u2)
                both = u1 + u2
                term = both * (2.0 * lattice(a, c) + both)
                growth = term if growth is None else growth + term
            g1, g2, g3 = pieces(growth, 3)
            minus_high = [-2.0 * v for v in high]
            minus_low = [-2.0 * v for v in low]
            row = (group * NB + a) * 80
            for n, value in enumerate([one, g3] + high + low + [g1, g2]):
                base_ref[row + n * 8 : row + n * 8 + 8, :] = value
            row = (group * NB + a) * 104
            for n, value in enumerate([g3, one] + minus_high + minus_low + minus_high + [zero, zero]):
                other_ref[row + n * 8 : row + n * 8 + 8, :] = value

    acc_ref[...] = jnp.zeros_like(acc_ref)

    tile_row = sublane_iota((BLK, BLK))
    tile_col = lane_iota((BLK, BLK))
    spread = jnp.where((tile_row & 15) == (tile_col >> 3), 1.0, 0.0).astype(BF16)
    own_lane = (lane >> 4) == sub

    def batch(step, carry):
        chosen = []
        for n in range(TILE_UNROLL):
            flat = step * TILE_UNROLL + n
            in_range = flat < count
            tile = list_ref[jnp.where(in_range, flat, 0)]
            grain, t = tile >> 2, tile & 3
            a = tiles_ref[t, 0, first_grain + grain]
            b = tiles_ref[t, 1, first_grain + grain]
            target = jnp.where(in_range, grain * NB + a, grains * NB)
            chosen.append((grain, t, a, b, target))

        def rows(ref, per, grain, a, first):
            start = ((grain >> 3) * NB + a) * (per * 8) + first * 8 + (grain & 7)
            return ref[pl.ds(start, 8, stride=8), :]

        def fixed(a):
            return fixed_ref[pl.ds(pl.multiple_of(a * 8, 8), 8), :]

        growths, words = [], []
        for grain, t, a, b, _ in chosen:
            base_a = rows(base_ref, 10, grain, a, 2)
            left = jnp.concatenate([base_a, fixed(a), rows(base_ref, 10, grain, a, 0), base_a], axis=0)
            right = jnp.concatenate(
                [
                    fixed(b),
                    rows(base_ref, 10, grain, b, 2),
                    rows(other_ref, 13, grain, b, 0),
                    rows(other_ref, 13, grain, b, 5),
                ],
                axis=0,
            ).astype(BF16)
            growths.append(jnp.dot(left.T.astype(BF16), right, preferred_element_type=F32))
            word = words_ref[pl.ds((first_grain + grain) * 64 + t, 16, stride=4), :].astype(F32)
            picked = jnp.concatenate(
                [jnp.where(own_lane, jnp.broadcast_to(word[r : r + 1, :], (8, BLK)), 0.0) for r in range(16)],
                axis=0,
            ).astype(BF16)
            words.append(jnp.dot(picked, spread, preferred_element_type=F32).astype(jnp.int32))
        pulls = []
        for (grain, t, a, b, _), growth, word in zip(chosen, growths, words):
            apart = jnp.clip(b - a, -REACH, REACH) + REACH
            table = pl.ds(pl.multiple_of(apart * BLK, BLK), BLK)
            live = (word & flag_ref[table, :]) == dead_ref[table, :]
            pull = inverse_rest_ref[table, :] - lax.rsqrt(rest_ref[table, :] + growth)
            pulls.append(jnp.where(live, pull, 0.0))
        forces = []
        for (grain, t, a, b, _), pull in zip(chosen, pulls):
            high, low = halves(pull)
            moments = jnp.concatenate([rows(base_ref, 10, grain, b, 2), fixed(b)], axis=0).astype(BF16)
            forces.append(
                lax.dot_general(
                    jnp.concatenate([high, low], axis=1),
                    jnp.concatenate([moments, moments], axis=1),
                    ACROSS,
                    preferred_element_type=F32,
                ).T
            )
        for (_, _, _, _, target), force in zip(chosen, forces):
            acc_ref[pl.ds(pl.multiple_of(target * 16, 16), 16), :] += force
        return carry

    lax.fori_loop(0, (count + TILE_UNROLL - 1) // TILE_UNROLL, batch, 0)

    for group in range(grains // 8):
        for a in range(NB):
            row = (group * 8 * NB + a) * 16
            acc = [acc_ref[pl.ds(row + n, 8, stride=NB * 16), :] for n in (0, 1, 2, 3, 4, 5, 8, 9, 10, 14)]
            base = (group * NB + a) * 80
            for c in range(3):
                own = lattice(a, c) + (
                    base_ref[base + 16 + 8 * c : base + 24 + 8 * c, :]
                    + base_ref[base + 40 + 8 * c : base + 48 + 8 * c, :]
                )
                force = acc[c] + acc[3 + c] - 0.5 * acc[6 + c] - acc[9] * own
                out_ref[c, 8 * group : 8 * group + 8, a * BLK : (a + 1) * BLK] = force * BOND_STIFF


def bond_forces(first_grain, grains, tile_list, displacement, words):
    vmem = pl.BlockSpec(memory_space=pltpu.VMEM)
    smem = pl.BlockSpec(memory_space=pltpu.SMEM)
    blocks = grains * NB
    table = (2 * REACH + 1) * BLK
    return pl.pallas_call(
        functools.partial(bond_kernel, first_grain, grains),
        out_shape=jax.ShapeDtypeStruct((3, grains, NODES), F32),
        in_specs=[smem, vmem, vmem],
        out_specs=vmem,
        scratch_shapes=[
            pltpu.VMEM((blocks * 10, BLK), F32),
            pltpu.VMEM((blocks * 13, BLK), F32),
            pltpu.VMEM((NB * 8, BLK), F32),
            pltpu.VMEM((table, BLK), F32),
            pltpu.VMEM((table, BLK), F32),
            pltpu.VMEM((table, BLK), jnp.int32),
            pltpu.VMEM((table, BLK), jnp.int32),
            pltpu.VMEM(((blocks + 1) * 16, BLK), F32),
            pltpu.SMEM((grains * TILES + 1,), jnp.int32),
        ],
        compiler_params=pltpu.CompilerParams(vmem_limit_bytes=24 * MIB),
        cost_estimate=pl.CostEstimate(flops=2_000_000_000, transcendentals=2_000_000, bytes_accessed=2_000_000),
        name="bond_forces",
    )(tile_list, displacement, words)


def inverse_kernel(nodes_ref, out_ref):
    sub128 = sublane_iota((BLK, SB * BLK))
    sub16 = sublane_iota((16, SB * BLK))
    k_index = lane_iota((16, SB * BLK))
    k_value = jnp.where(sub16 < 8, k_index & 127, 1 + (k_index >> 7)).astype(F32)

    def step(part, carry):
        for n in range(8):
            grain = part * 8 + n
            node = nodes_ref[pl.ds(grain, 1), :]
            hit = jnp.where(jnp.broadcast_to(node & 127, (BLK, SB * BLK)) == sub128, 1.0, 0.0).astype(BF16)
            block = jnp.broadcast_to(node >> 7, (16, SB * BLK))
            value = jnp.where(block == (sub16 & 7), k_value, 0.0).astype(BF16)
            out_ref[pl.ds(pl.multiple_of(grain * 16, 16), 16), :] = lax.dot_general(
                value, hit, ACROSS, preferred_element_type=F32
            )
        return carry

    lax.fori_loop(0, GRAINS_DEV // 8, step, 0)


def surface_places(surface_nodes):
    vmem = pl.BlockSpec(memory_space=pltpu.VMEM)
    return pl.pallas_call(
        inverse_kernel,
        out_shape=jax.ShapeDtypeStruct((GRAINS_DEV * 16, BLK), F32),
        in_specs=[vmem],
        out_specs=vmem,
        compiler_params=pltpu.CompilerParams(vmem_limit_bytes=8 * MIB),
        cost_estimate=pl.CostEstimate(flops=500_000_000, transcendentals=0, bytes_accessed=500_000),
        name="surface_places",
    )(surface_nodes)


def sum_kernel(bonds, send_ref, back_ref, inverse_ref, vel_ref, *refs):
    bond_refs, (force_ref, new_ref, block_ref) = refs[:bonds], refs[bonds:]
    for d in range(SLOTS):
        block = send_ref[0, d]
        grain = block >> 2
        row = ((grain >> 3) * SB + (block & 3)) * 24 + (grain & 7)
        block_ref[pl.ds(row, 3, stride=8), :] = back_ref[3 * d : 3 * d + 3, :]
    for group in range(GROUPS):
        grains = pl.ds(8 * group, 8)
        bond_ref = bond_refs[group * bonds // GROUPS]
        bond_grains = pl.ds((8 * group) % (GRAINS_DEV // bonds), 8)
        for a in range(NB):
            lane = inverse_ref[pl.ds(group * 128 + a, 8, stride=16), :].astype(jnp.int32)
            block = inverse_ref[pl.ds(group * 128 + 8 + a, 8, stride=16), :].astype(jnp.int32)
            columns = slice(a * BLK, (a + 1) * BLK)
            for c in range(3):
                value = jnp.zeros((8, BLK), F32)
                for k in range(SB):
                    start = (group * SB + k) * 24 + c * 8
                    value = jnp.where(block == k + 1, lane_gather(block_ref[start : start + 8, :], lane), value)
                force = bond_ref[c, bond_grains, columns] + value
                force_ref[c, grains, columns] = force
                new_ref[c, grains, columns] = vel_ref[c, grains, columns] + TIME_STEP * force


def sum_forces(send_order, returned, inverse, velocity, bonds):
    vmem = pl.BlockSpec(memory_space=pltpu.VMEM)
    shape = jax.ShapeDtypeStruct((3, GRAINS_DEV, NODES), F32)
    return pl.pallas_call(
        functools.partial(sum_kernel, len(bonds)),
        out_shape=(shape, shape),
        in_specs=[pl.BlockSpec(memory_space=pltpu.SMEM)] + [vmem] * (3 + len(bonds)),
        out_specs=(vmem, vmem),
        scratch_shapes=[pltpu.VMEM((SLOTS * 3, BLK), F32)],
        compiler_params=pltpu.CompilerParams(vmem_limit_bytes=8 * MIB),
        name="sum_forces",
    )(send_order, returned, inverse, velocity, *bonds)


def exchange(rows, width):
    moved = lax.all_to_all(
        rows.reshape(SLOTS, 1, width, BLK), ("grain", "cell"), split_axis=0, concat_axis=0, tiled=True
    )
    return moved.reshape(SLOTS * width, BLK)


def on_device(
    displacement,
    velocity,
    centers,
    tile_list,
    broken_bits,
    surface_nodes,
    send_order,
    pair_list,
    pair_count,
):
    displacement = displacement.transpose(1, 0, 2)
    velocity = velocity.transpose(1, 0, 2)
    tiles = tile_list.transpose(1, 2, 0)
    pairs = pair_list[0].T
    words = broken_bits.reshape(GRAINS_DEV, TILES, 16, BLK).transpose(0, 2, 1, 3).reshape(GRAINS_DEV * 64, BLK)
    outgoing = surface_blocks(send_order, displacement, velocity, centers, surface_nodes)
    received = exchange(outgoing, 6)
    half = GRAINS_DEV // 2
    bonds = [bond_forces(first, half, tiles, displacement, words) for first in (0, half)]
    inverse = surface_places(surface_nodes)
    received, bonds[0] = lax.optimization_barrier((received, bonds[0]))
    slot_force = contact_forces(pair_count, pairs, received)
    returned = exchange(slot_force, 3)
    force, new_velocity = sum_forces(send_order, returned, inverse, velocity, bonds)
    return force.transpose(1, 0, 2), new_velocity.transpose(1, 0, 2)


def solution(mesh):
    return jax.shard_map(
        on_device,
        mesh=mesh,
        in_specs=(
            P(("grain", "cell"), None, None),
            P(("grain", "cell"), None, None),
            P(None, ("grain", "cell")),
            P(("grain", "cell"), None, None),
            P(("grain", "cell"), None, None),
            P(("grain", "cell"), None),
            P(("grain", "cell"), None),
            P(("grain", "cell"), None, None),
            P(("grain", "cell")),
        ),
        out_specs=(P(("grain", "cell"), None, None), P(("grain", "cell"), None, None)),
        check_vma=False,
    )
```

```python
import functools
import math

import jax
import jax.numpy as jnp
from jax import lax
from jax.experimental import pallas as pl
from jax.experimental.pallas import tpu as pltpu
from jax.sharding import PartitionSpec as P

BLK = 128
SB = 4
GRAINS_DEV = 32
NODES = 768
NB = NODES // BLK
SLOTS = 128
GROUPS = GRAINS_DEV // 8

CONTACT_STIFF = 0.02
CONTACT_DAMP = 0.05
CONTACT_RANGE = 9.0
TIME_STEP = 0.5
BOND_STIFF = 5.0
HORIZON = 3.0
ORIGIN = (3.5, 3.5, 5.5)
LANE = 1
F32 = jnp.float32
BF16 = jnp.bfloat16
MIB = 1 << 20
REACH = 2
ACROSS = (((1,), (1,)), ((), ()))
DOWN = (((1,), (0,)), ((), ()))
ALONG = (((0,), (0,)), ((), ()))


def pieces(value, count):
    parts = []
    rest = value
    for step in range(count):
        head = rest.astype(BF16).astype(F32)
        parts.append(head)
        if step + 1 < count:
            rest = rest - head
    return parts


def halves(value):
    high = value.astype(BF16)
    return high, (value - high.astype(F32)).astype(BF16)


def lane_gather(source, index):
    return jnp.take_along_axis(source, index, axis=1, mode="promise_in_bounds")


def lane_iota(shape):
    return lax.broadcasted_iota(jnp.int32, shape, len(shape) - 1)


def sublane_iota(shape):
    return lax.broadcasted_iota(jnp.int32, shape, 0)


def gather_kernel(
    send_hbm,
    disp_hbm,
    vel_hbm,
    centers_hbm,
    nodes_hbm,
    out_hbm,
    send_ref,
    disp_ref,
    vel_ref,
    centers_ref,
    nodes_ref,
    state_ref,
    out_ref,
    sems,
    group_sems,
    out_sems,
):
    small = [
        pltpu.make_async_copy(centers_hbm, centers_ref, sems.at[0]),
        pltpu.make_async_copy(send_hbm, send_ref, sems.at[1]),
    ]
    large = []
    for group in range(GROUPS):
        these = pl.ds(8 * group, 8)
        large.append(
            [
                pltpu.make_async_copy(nodes_hbm.at[these], nodes_ref.at[these], group_sems.at[group, 0]),
                pltpu.make_async_copy(disp_hbm.at[:, these], disp_ref.at[:, these], group_sems.at[group, 1]),
                pltpu.make_async_copy(vel_hbm.at[:, these], vel_ref.at[:, these], group_sems.at[group, 2]),
            ]
        )
    small[0].start()
    for copies in large:
        for copy in copies:
            copy.start()
    small[1].start()
    small[0].wait()
    for group in range(GROUPS):
        grains = pl.ds(8 * group, 8)
        own = lane_iota((8, GRAINS_DEV)) == sublane_iota((8, GRAINS_DEV)) + 8 * group
        offsets = [
            jnp.sum(
                jnp.where(own, jnp.broadcast_to(centers_ref[c : c + 1, :], own.shape), 0.0),
                axis=1,
                keepdims=True,
            )
            for c in range(3)
        ]
        for copy in large[group]:
            copy.wait()
        for k in range(SB):
            node = nodes_ref[grains, k * BLK : (k + 1) * BLK]
            lane = node & (BLK - 1)
            block = node >> 7
            rest = (node & 7, (node >> 3) & 7, node >> 6)
            for c in range(6):
                ref = disp_ref if c < 3 else vel_ref
                value = lane_gather(ref[c % 3, grains, :BLK], lane)
                for a in range(1, NB):
                    source = ref[c % 3, grains, a * BLK : (a + 1) * BLK]
                    value = jnp.where(block == a, lane_gather(source, lane), value)
                if c < 3:
                    value = rest[c].astype(F32) + value + offsets[c]
                state_ref[pl.ds((group * SB + k) * 48 + c * 8, 8), :] = value
    small[1].wait()
    done = []
    for d in range(SLOTS):
        block = send_ref[0, d]
        grain = block >> 2
        row = ((grain >> 3) * SB + (block & 3)) * 48 + (grain & 7)
        out_ref[6 * d : 6 * d + 6, :] = state_ref[pl.ds(row, 6, stride=8), :]
        if d % 32 == 31:
            part = pl.ds(6 * (d - 31), 192)
            done.append(pltpu.make_async_copy(out_ref.at[part], out_hbm.at[part], out_sems.at[d // 32]))
            done[-1].start()
    for copy in done:
        copy.wait()


def surface_blocks(send_order, displacement, velocity, centers, surface_nodes):
    hbm = pl.BlockSpec(memory_space=pltpu.HBM)
    return pl.pallas_call(
        gather_kernel,
        out_shape=jax.ShapeDtypeStruct((SLOTS * 6, BLK), F32),
        in_specs=[hbm] * 5,
        out_specs=hbm,
        scratch_shapes=[
            pltpu.SMEM((1, SLOTS), jnp.int32),
            pltpu.VMEM((3, GRAINS_DEV, NODES), F32),
            pltpu.VMEM((3, GRAINS_DEV, NODES), F32),
            pltpu.VMEM((3, GRAINS_DEV), F32),
            pltpu.VMEM((GRAINS_DEV, SB * BLK), jnp.int32),
            pltpu.VMEM((SLOTS * 6, BLK), F32),
            pltpu.VMEM((SLOTS * 6, BLK), F32),
            pltpu.SemaphoreType.DMA((2,)),
            pltpu.SemaphoreType.DMA((GROUPS, 3)),
            pltpu.SemaphoreType.DMA((GROUPS,)),
        ],
        compiler_params=pltpu.CompilerParams(vmem_limit_bytes=60 * MIB),
        name="surface_blocks",
    )(send_order, displacement, velocity, centers, surface_nodes)


PAIR_UNROLL = 32


def contact_kernel(
    lists_hbm,
    state_ref,
    out_hbm,
    lists_ref,
    left_ref,
    right_ref,
    slide_ref,
    acc_ref,
    out_ref,
    sem,
    out_sems,
):
    fetch = pltpu.make_async_copy(lists_hbm, lists_ref, sem)
    fetch.start()
    scale = math.log2(math.e) / CONTACT_RANGE
    one = jnp.ones((8, BLK), F32)
    pad = jnp.zeros((8, BLK), F32)

    def put(ref, rows, group, values):
        for n, value in enumerate(values):
            ref[pl.ds(pl.multiple_of(group * (rows * 8) + n * 8, 8), 8), :] = value

    def prepare(group, carry):
        first = group * 48
        place = [state_ref[pl.ds(first + c, 8, stride=6), :] - ORIGIN[c] for c in range(3)]
        speed = [state_ref[pl.ds(first + 3 + c, 8, stride=6), :] for c in range(3)]
        norm = place[0] * place[0] + place[1] * place[1] + place[2] * place[2]
        norm = pieces(-scale * norm, 3)
        left, right, slide = [], [], []
        for c in range(3):
            p1, p2, p3 = pieces(place[c], 3)
            q1, q2, q3 = pieces(place[c] * (2.0 * scale), 3)
            left += [p1, p1, p2, p2, p1, p3]
            right += [q1, q2, q1, q2, q3, q1]
        left += norm + [one] * 3
        right += [one] * 3 + norm
        for c in range(3):
            slide += pieces(CONTACT_STIFF * place[c] - CONTACT_DAMP * speed[c], 3)
        slide += [one]
        put(left_ref, 24, group, left)
        put(right_ref, 24, group, right)
        put(slide_ref, 16, group, slide)
        return carry

    lax.fori_loop(0, SLOTS // 8, prepare, 0, unroll=4)
    acc_ref[...] = jnp.zeros_like(acc_ref)
    fetch.wait()
    total = lists_ref[2, 0]

    def rows(ref, count, slot):
        return ref[pl.ds((slot >> 3) * (count * 8) + (slot & 7), count, stride=8), :]

    def batch(step, carry):
        chosen = []
        for n in range(PAIR_UNROLL):
            flat = step * PAIR_UNROLL + n
            in_range = flat < total
            at = jnp.minimum(flat, SLOTS - 1)
            i = jnp.where(in_range, lists_ref[0, at], 0)
            j = jnp.where(in_range, lists_ref[1, at], 0)
            chosen.append((i, j, jnp.where(in_range, i, SLOTS), jnp.where(in_range, j, SLOTS)))
        weights = []
        for i, j, _, _ in chosen:
            left = jnp.concatenate([rows(left_ref, 24, i), pad], axis=0).astype(BF16)
            right = jnp.concatenate([rows(right_ref, 24, j), pad], axis=0).astype(BF16)
            exponent = lax.dot_general(left, right, ALONG, preferred_element_type=F32)
            weights.append(jnp.exp2(exponent))
        sums = []
        for (i, j, _, _), weight in zip(chosen, weights):
            slide_i = rows(slide_ref, 16, i).astype(BF16)
            slide_j = rows(slide_ref, 16, j).astype(BF16)
            to_i = lax.dot_general(
                jnp.concatenate([slide_j, slide_j], axis=1),
                jnp.concatenate(halves(weight.T), axis=0),
                DOWN,
                preferred_element_type=F32,
            )
            to_j = lax.dot_general(
                jnp.concatenate([slide_i, slide_i], axis=1),
                jnp.concatenate(halves(weight), axis=0),
                DOWN,
                preferred_element_type=F32,
            )
            sums.append((to_i, to_j))
        for (_, _, i, j), (to_i, to_j) in zip(chosen, sums):
            rows_i = pl.ds(pl.multiple_of(i * 16, 16), 16)
            acc_ref[rows_i, :] += to_i
            rows_j = pl.ds(pl.multiple_of(j * 16, 16), 16)
            acc_ref[rows_j, :] += to_j
        return carry

    lax.fori_loop(0, (total + PAIR_UNROLL - 1) // PAIR_UNROLL, batch, 0)

    def finish(group):
        def acc(n):
            return acc_ref[pl.ds(group * 128 + n, 8, stride=16), :]

        def slide(n):
            return slide_ref[group * 128 + n * 8 : group * 128 + n * 8 + 8, :]

        total_weight = acc(9)
        for c in range(3):
            own = slide(3 * c) + slide(3 * c + 1) + slide(3 * c + 2)
            other = acc(3 * c) + acc(3 * c + 1) + acc(3 * c + 2)
            out_ref[pl.ds(group * 24 + c, 8, stride=3), :] = own * total_weight - other

    done = []
    for group in range(SLOTS // 8):
        finish(group)
        if group % 4 == 3:
            part = pl.ds(24 * (group - 3), 96)
            done.append(pltpu.make_async_copy(out_ref.at[part], out_hbm.at[part], out_sems.at[group // 4]))
            done[-1].start()
    for copy in done:
        copy.wait()


def contact_forces(lists, state):
    vmem = pl.BlockSpec(memory_space=pltpu.VMEM)
    hbm = pl.BlockSpec(memory_space=pltpu.HBM)
    return pl.pallas_call(
        contact_kernel,
        out_shape=jax.ShapeDtypeStruct((SLOTS * 3, BLK), F32),
        in_specs=[pl.BlockSpec(memory_space=pl.ANY), vmem],
        out_specs=hbm,
        scratch_shapes=[
            pltpu.SMEM((8, SLOTS), jnp.int32),
            pltpu.VMEM((SLOTS * 24, BLK), F32),
            pltpu.VMEM((SLOTS * 24, BLK), F32),
            pltpu.VMEM((SLOTS * 16, BLK), F32),
            pltpu.VMEM(((SLOTS + 1) * 16, BLK), F32),
            pltpu.VMEM((SLOTS * 3, BLK), F32),
            pltpu.SemaphoreType.DMA,
            pltpu.SemaphoreType.DMA((4,)),
        ],
        compiler_params=pltpu.CompilerParams(vmem_limit_bytes=24 * MIB),
        name="contact_forces",
    )(lists, state)


TILE_UNROLL = 16
TILES = 4
BOND_PARTS = ((0, 8), (8, 24))


def bond_kernel(
    first_grain,
    grains,
    tiles_ref,
    disp_ref,
    words_ref,
    out_ref,
    base_ref,
    other_ref,
    fixed_ref,
    rest_ref,
    inverse_rest_ref,
    flag_ref,
    dead_ref,
    acc_ref,
    list_ref,
):
    lane = lane_iota((8, BLK))
    sub = sublane_iota((8, BLK))
    one = jnp.ones((8, BLK), F32)
    zero = jnp.zeros((8, BLK), F32)

    def lattice(a, c):
        index = lane + a * BLK
        return ((index & 7, (index >> 3) & 7, index >> 6)[c]).astype(F32) - ORIGIN[c]

    count = jnp.int32(0)
    for grain in range(grains):
        for t in range(TILES):
            apart = tiles_ref[t, 0, first_grain + grain] - tiles_ref[t, 1, first_grain + grain]
            list_ref[count] = grain * TILES + t
            count += jnp.where((apart >= -REACH) & (apart <= REACH), 1, 0)

    for a in range(NB):
        rows = jnp.where(sub < 6, 0.0, 1.0)
        for c in range(3):
            rows = jnp.where((sub == c) | (sub == c + 3), -2.0 * lattice(a, c), rows)
        fixed_ref[a * 8 : a * 8 + 8, :] = rows

    col_y = (lane >> 3) & 7
    for apart in range(-REACH, REACH + 1):
        for r in range(16):
            dx = sub - (lane & 7)
            dy = (r & 7) - col_y
            dz = (r >> 3) - (lane >> 6) - 2 * apart
            square = dx * dx + dy * dy + dz * dz
            near = (square >= 1) & (square <= 9)
            row = ((apart + REACH) * 16 + r) * 8
            rest = square.astype(F32)
            rest_ref[row : row + 8, :] = rest
            inverse_rest_ref[row : row + 8, :] = lax.rsqrt(jnp.maximum(rest, 1.0))
            flag_ref[row : row + 8, :] = jnp.where(near, jnp.left_shift(1, lane & 7), 0)
            dead_ref[row : row + 8, :] = jnp.where(near, 0, 1)

    for group in range(grains // 8):
        these = pl.ds(first_grain + 8 * group, 8)
        for a in range(NB):
            high, low, growth = [], [], None
            for c in range(3):
                u1, u2 = pieces(disp_ref[c, these, a * BLK : (a + 1) * BLK], 2)
                high.append(u1)
                low.append(u2)
                both = u1 + u2
                term = both * (2.0 * lattice(a, c) + both)
                growth = term if growth is None else growth + term
            g1, g2, g3 = pieces(growth, 3)
            minus_high = [-2.0 * v for v in high]
            minus_low = [-2.0 * v for v in low]
            row = (group * NB + a) * 80
            for n, value in enumerate([one, g3] + high + low + [g1, g2]):
                base_ref[row + n * 8 : row + n * 8 + 8, :] = value
            row = (group * NB + a) * 104
            for n, value in enumerate([g3, one] + minus_high + minus_low + minus_high + [zero, zero]):
                other_ref[row + n * 8 : row + n * 8 + 8, :] = value

    acc_ref[...] = jnp.zeros_like(acc_ref)

    tile_row = sublane_iota((BLK, BLK))
    tile_col = lane_iota((BLK, BLK))
    spread = jnp.where((tile_row & 15) == (tile_col >> 3), 1.0, 0.0).astype(BF16)
    own_lane = (lane >> 4) == sub

    def batch(step, carry):
        chosen = []
        for n in range(TILE_UNROLL):
            flat = step * TILE_UNROLL + n
            in_range = flat < count
            tile = list_ref[jnp.where(in_range, flat, 0)]
            grain, t = tile >> 2, tile & 3
            a = tiles_ref[t, 0, first_grain + grain]
            b = tiles_ref[t, 1, first_grain + grain]
            target = jnp.where(in_range, grain * NB + a, grains * NB)
            chosen.append((grain, t, a, b, target))

        def rows(ref, per, grain, a, first):
            start = ((grain >> 3) * NB + a) * (per * 8) + first * 8 + (grain & 7)
            return ref[pl.ds(start, 8, stride=8), :]

        def fixed(a):
            return fixed_ref[pl.ds(pl.multiple_of(a * 8, 8), 8), :]

        growths, words = [], []
        for grain, t, a, b, _ in chosen:
            base_a = rows(base_ref, 10, grain, a, 2)
            left = jnp.concatenate([base_a, fixed(a), rows(base_ref, 10, grain, a, 0), base_a], axis=0)
            right = jnp.concatenate(
                [
                    fixed(b),
                    rows(base_ref, 10, grain, b, 2),
                    rows(other_ref, 13, grain, b, 0),
                    rows(other_ref, 13, grain, b, 5),
                ],
                axis=0,
            ).astype(BF16)
            growths.append(jnp.dot(left.T.astype(BF16), right, preferred_element_type=F32))
            word = words_ref[pl.ds((first_grain + grain) * 64 + t, 16, stride=4), :].astype(F32)
            picked = jnp.concatenate(
                [jnp.where(own_lane, jnp.broadcast_to(word[r : r + 1, :], (8, BLK)), 0.0) for r in range(16)],
                axis=0,
            ).astype(BF16)
            words.append(jnp.dot(picked, spread, preferred_element_type=F32).astype(jnp.int32))
        pulls = []
        for (grain, t, a, b, _), growth, word in zip(chosen, growths, words):
            apart = jnp.clip(b - a, -REACH, REACH) + REACH
            table = pl.ds(pl.multiple_of(apart * BLK, BLK), BLK)
            live = (word & flag_ref[table, :]) == dead_ref[table, :]
            pull = inverse_rest_ref[table, :] - lax.rsqrt(rest_ref[table, :] + growth)
            pulls.append(jnp.where(live, pull, 0.0))
        forces = []
        for (grain, t, a, b, _), pull in zip(chosen, pulls):
            high, low = halves(pull)
            moments = jnp.concatenate([rows(base_ref, 10, grain, b, 2), fixed(b)], axis=0).astype(BF16)
            forces.append(
                lax.dot_general(
                    jnp.concatenate([high, low], axis=1),
                    jnp.concatenate([moments, moments], axis=1),
                    ACROSS,
                    preferred_element_type=F32,
                ).T
            )
        for (_, _, _, _, target), force in zip(chosen, forces):
            acc_ref[pl.ds(pl.multiple_of(target * 16, 16), 16), :] += force
        return carry

    lax.fori_loop(0, (count + TILE_UNROLL - 1) // TILE_UNROLL, batch, 0)

    for group in range(grains // 8):
        for a in range(NB):
            row = (group * 8 * NB + a) * 16
            acc = [acc_ref[pl.ds(row + n, 8, stride=NB * 16), :] for n in (0, 1, 2, 3, 4, 5, 8, 9, 10, 14)]
            base = (group * NB + a) * 80
            for c in range(3):
                own = lattice(a, c) + (
                    base_ref[base + 16 + 8 * c : base + 24 + 8 * c, :]
                    + base_ref[base + 40 + 8 * c : base + 48 + 8 * c, :]
                )
                force = acc[c] + acc[3 + c] - 0.5 * acc[6 + c] - acc[9] * own
                out_ref[c, 8 * group : 8 * group + 8, a * BLK : (a + 1) * BLK] = force * BOND_STIFF


def bond_forces(first_grain, grains, tile_list, displacement, words):
    vmem = pl.BlockSpec(memory_space=pltpu.VMEM)
    smem = pl.BlockSpec(memory_space=pltpu.SMEM)
    blocks = grains * NB
    table = (2 * REACH + 1) * BLK
    return pl.pallas_call(
        functools.partial(bond_kernel, first_grain, grains),
        out_shape=jax.ShapeDtypeStruct((3, grains, NODES), F32),
        in_specs=[smem, vmem, vmem],
        out_specs=vmem,
        scratch_shapes=[
            pltpu.VMEM((blocks * 10, BLK), F32),
            pltpu.VMEM((blocks * 13, BLK), F32),
            pltpu.VMEM((NB * 8, BLK), F32),
            pltpu.VMEM((table, BLK), F32),
            pltpu.VMEM((table, BLK), F32),
            pltpu.VMEM((table, BLK), jnp.int32),
            pltpu.VMEM((table, BLK), jnp.int32),
            pltpu.VMEM(((blocks + 1) * 16, BLK), F32),
            pltpu.SMEM((grains * TILES + 1,), jnp.int32),
        ],
        compiler_params=pltpu.CompilerParams(vmem_limit_bytes=24 * MIB),
        cost_estimate=pl.CostEstimate(flops=2_000_000_000, transcendentals=2_000_000, bytes_accessed=2_000_000),
        name="bond_forces",
    )(tile_list, displacement, words)


def inverse_kernel(count_ref, nodes_ref, pairs_ref, send_ref, out_ref, lists_ref):
    lists_ref[:2, :] = pairs_ref[...]
    lists_ref[2:3, :] = jnp.full((1, SLOTS), count_ref[0], jnp.int32)
    lists_ref[3:4, :] = send_ref[...]
    lists_ref[4:, :] = jnp.zeros((4, SLOTS), jnp.int32)
    sub128 = sublane_iota((BLK, SB * BLK))
    sub16 = sublane_iota((16, SB * BLK))
    k_index = lane_iota((16, SB * BLK))
    k_value = jnp.where(sub16 < 8, k_index & 127, 1 + (k_index >> 7)).astype(F32)

    def step(part, carry):
        for n in range(8):
            grain = part * 8 + n
            node = nodes_ref[pl.ds(grain, 1), :]
            hit = jnp.where(jnp.broadcast_to(node & 127, (BLK, SB * BLK)) == sub128, 1.0, 0.0).astype(BF16)
            block = jnp.broadcast_to(node >> 7, (16, SB * BLK))
            value = jnp.where(block == (sub16 & 7), k_value, 0.0).astype(BF16)
            out_ref[pl.ds(pl.multiple_of(grain * 16, 16), 16), :] = lax.dot_general(
                value, hit, ACROSS, preferred_element_type=F32
            )
        return carry

    lax.fori_loop(0, GRAINS_DEV // 8, step, 0)


def surface_places(pair_count, surface_nodes, pairs, send_order):
    vmem = pl.BlockSpec(memory_space=pltpu.VMEM)
    return pl.pallas_call(
        inverse_kernel,
        out_shape=(
            jax.ShapeDtypeStruct((GRAINS_DEV * 16, BLK), F32),
            jax.ShapeDtypeStruct((8, SLOTS), jnp.int32),
        ),
        in_specs=[pl.BlockSpec(memory_space=pltpu.SMEM), vmem, vmem, vmem],
        out_specs=(vmem, vmem),
        compiler_params=pltpu.CompilerParams(vmem_limit_bytes=8 * MIB),
        cost_estimate=pl.CostEstimate(flops=500_000_000, transcendentals=0, bytes_accessed=500_000),
        name="surface_places",
    )(pair_count, surface_nodes, pairs, send_order)


def sum_kernel(bonds, lists_hbm, back_ref, inverse_ref, vel_ref, *refs):
    bond_refs = refs[:bonds]
    force_hbm, new_hbm, lists_ref, force_ref, new_ref, block_ref, lists_sem, out_sems = refs[bonds:]
    fetch = pltpu.make_async_copy(lists_hbm, lists_ref, lists_sem)
    fetch.start()
    places = []
    for group in range(GROUPS):
        for a in range(NB):
            lane = inverse_ref[pl.ds(group * 128 + a, 8, stride=16), :].astype(jnp.int32)
            block = inverse_ref[pl.ds(group * 128 + 8 + a, 8, stride=16), :].astype(jnp.int32)
            places.append((lane, block))
    fetch.wait()
    for d in range(SLOTS):
        block = lists_ref[3, d]
        grain = block >> 2
        row = ((grain >> 3) * SB + (block & 3)) * 24 + (grain & 7)
        block_ref[pl.ds(row, 3, stride=8), :] = back_ref[3 * d : 3 * d + 3, :]
    done = []
    for group in range(GROUPS):
        grains = pl.ds(8 * group, 8)
        part = max(n for n in range(bonds) if BOND_PARTS[n][0] <= 8 * group)
        bond_ref = bond_refs[part]
        bond_grains = pl.ds(8 * group - BOND_PARTS[part][0], 8)
        for a in range(NB):
            lane, block = places[group * NB + a]
            columns = slice(a * BLK, (a + 1) * BLK)
            for c in range(3):
                value = jnp.zeros((8, BLK), F32)
                for k in range(SB):
                    start = (group * SB + k) * 24 + c * 8
                    value = jnp.where(block == k + 1, lane_gather(block_ref[start : start + 8, :], lane), value)
                force = bond_ref[c, bond_grains, columns] + value
                force_ref[c, grains, columns] = force
                new_ref[c, grains, columns] = vel_ref[c, grains, columns] + TIME_STEP * force
        for n, (source, target) in enumerate(((force_ref, force_hbm), (new_ref, new_hbm))):
            done.append(pltpu.make_async_copy(source.at[:, grains], target.at[:, grains], out_sems.at[group, n]))
            done[-1].start()
    for copy in done:
        copy.wait()


def sum_forces(lists, returned, inverse, velocity, bonds):
    vmem = pl.BlockSpec(memory_space=pltpu.VMEM)
    hbm = pl.BlockSpec(memory_space=pltpu.HBM)
    shape = (3, GRAINS_DEV, NODES)
    return pl.pallas_call(
        functools.partial(sum_kernel, len(bonds)),
        out_shape=(jax.ShapeDtypeStruct(shape, F32),) * 2,
        in_specs=[pl.BlockSpec(memory_space=pl.ANY)] + [vmem] * (3 + len(bonds)),
        out_specs=(hbm, hbm),
        scratch_shapes=[
            pltpu.SMEM((8, SLOTS), jnp.int32),
            pltpu.VMEM(shape, F32),
            pltpu.VMEM(shape, F32),
            pltpu.VMEM((SLOTS * 3, BLK), F32),
            pltpu.SemaphoreType.DMA,
            pltpu.SemaphoreType.DMA((GROUPS, 2)),
        ],
        compiler_params=pltpu.CompilerParams(vmem_limit_bytes=8 * MIB),
        name="sum_forces",
    )(lists, returned, inverse, velocity, *bonds)


def exchange(rows, width):
    moved = lax.all_to_all(
        rows.reshape(SLOTS, 1, width, BLK), ("grain", "cell"), split_axis=0, concat_axis=0, tiled=True
    )
    return moved.reshape(SLOTS * width, BLK)


def on_device(
    displacement,
    velocity,
    centers,
    tile_list,
    broken_bits,
    surface_nodes,
    send_order,
    pair_list,
    pair_count,
):
    displacement = displacement.transpose(1, 0, 2)
    velocity = velocity.transpose(1, 0, 2)
    tiles = tile_list.transpose(1, 2, 0)
    words = broken_bits.reshape(GRAINS_DEV, TILES, 16, BLK).transpose(0, 2, 1, 3).reshape(GRAINS_DEV * 64, BLK)
    outgoing = surface_blocks(send_order, displacement, velocity, centers, surface_nodes)
    received = exchange(outgoing, 6)
    inverse, lists = surface_places(pair_count, surface_nodes, pair_list[0].T, send_order)
    bonds = [bond_forces(first, count, tiles, displacement, words) for first, count in BOND_PARTS]
    received, lists, bonds[0] = lax.optimization_barrier((received, lists, bonds[0]))
    slot_force = contact_forces(lists, received)
    returned = exchange(slot_force, 3)
    force, new_velocity = sum_forces(lists, returned, inverse, velocity, bonds)
    return force.transpose(1, 0, 2), new_velocity.transpose(1, 0, 2)


def solution(mesh):
    return jax.shard_map(
        on_device,
        mesh=mesh,
        in_specs=(
            P(("grain", "cell"), None, None),
            P(("grain", "cell"), None, None),
            P(None, ("grain", "cell")),
            P(("grain", "cell"), None, None),
            P(("grain", "cell"), None, None),
            P(("grain", "cell"), None),
            P(("grain", "cell"), None),
            P(("grain", "cell"), None, None),
            P(("grain", "cell")),
        ),
        out_specs=(P(("grain", "cell"), None, None), P(("grain", "cell"), None, None)),
        check_vma=False,
    )
```

```python
import functools
import math

import jax
import jax.numpy as jnp
from jax import lax
from jax.experimental import pallas as pl
from jax.experimental.pallas import tpu as pltpu
from jax.sharding import PartitionSpec as P

BLK = 128
SB = 4
GRAINS_DEV = 32
NODES = 768
NB = NODES // BLK
SLOTS = 128
GROUPS = GRAINS_DEV // 8

CONTACT_STIFF = 0.02
CONTACT_DAMP = 0.05
CONTACT_RANGE = 9.0
TIME_STEP = 0.5
BOND_STIFF = 5.0
HORIZON = 3.0
ORIGIN = (3.5, 3.5, 5.5)
LANE = 1
F32 = jnp.float32
BF16 = jnp.bfloat16
MIB = 1 << 20
REACH = 2
ACROSS = (((1,), (1,)), ((), ()))
DOWN = (((1,), (0,)), ((), ()))
ALONG = (((0,), (0,)), ((), ()))


def pieces(value, count):
    parts = []
    rest = value
    for step in range(count):
        head = rest.astype(BF16).astype(F32)
        parts.append(head)
        if step + 1 < count:
            rest = rest - head
    return parts


def halves(value):
    high = value.astype(BF16)
    return high, (value - high.astype(F32)).astype(BF16)


def lane_gather(source, index):
    return jnp.take_along_axis(source, index, axis=1, mode="promise_in_bounds")


def lane_iota(shape):
    return lax.broadcasted_iota(jnp.int32, shape, len(shape) - 1)


def sublane_iota(shape):
    return lax.broadcasted_iota(jnp.int32, shape, 0)


def gather_kernel(
    send_hbm,
    disp_hbm,
    vel_hbm,
    centers_hbm,
    nodes_hbm,
    out_hbm,
    send_ref,
    disp_ref,
    vel_ref,
    centers_ref,
    nodes_ref,
    state_ref,
    out_ref,
    sems,
    group_sems,
    out_sems,
):
    small = [
        pltpu.make_async_copy(centers_hbm, centers_ref, sems.at[0]),
        pltpu.make_async_copy(send_hbm, send_ref, sems.at[1]),
    ]
    large = []
    for group in range(GROUPS):
        these = pl.ds(8 * group, 8)
        large.append(
            [
                pltpu.make_async_copy(nodes_hbm.at[these], nodes_ref.at[these], group_sems.at[group, 0]),
                pltpu.make_async_copy(disp_hbm.at[:, these], disp_ref.at[:, these], group_sems.at[group, 1]),
                pltpu.make_async_copy(vel_hbm.at[:, these], vel_ref.at[:, these], group_sems.at[group, 2]),
            ]
        )
    small[0].start()
    for copies in large:
        for copy in copies:
            copy.start()
    small[1].start()
    small[0].wait()
    for group in range(GROUPS):
        grains = pl.ds(8 * group, 8)
        own = lane_iota((8, GRAINS_DEV)) == sublane_iota((8, GRAINS_DEV)) + 8 * group
        offsets = [
            jnp.sum(
                jnp.where(own, jnp.broadcast_to(centers_ref[c : c + 1, :], own.shape), 0.0),
                axis=1,
                keepdims=True,
            )
            for c in range(3)
        ]
        if group % 2 == 0:
            for copy in large[group] + large[group + 1]:
                copy.wait()
        for k in range(SB):
            node = nodes_ref[grains, k * BLK : (k + 1) * BLK]
            lane = node & (BLK - 1)
            block = node >> 7
            rest = (node & 7, (node >> 3) & 7, node >> 6)
            for c in range(6):
                ref = disp_ref if c < 3 else vel_ref
                value = lane_gather(ref[c % 3, grains, :BLK], lane)
                for a in range(1, NB):
                    source = ref[c % 3, grains, a * BLK : (a + 1) * BLK]
                    value = jnp.where(block == a, lane_gather(source, lane), value)
                if c < 3:
                    value = rest[c].astype(F32) + value + offsets[c]
                state_ref[pl.ds(group * 256 + k * 8 + c, 8, stride=32), :] = value
    small[1].wait()
    done = []
    for d in range(SLOTS):
        row = pl.multiple_of(send_ref[0, d] * 8, 8)
        out_ref[6 * d : 6 * d + 6, :] = state_ref[pl.ds(row, 8), :][:6]
        if d % 32 == 31:
            part = pl.ds(6 * (d - 31), 192)
            done.append(pltpu.make_async_copy(out_ref.at[part], out_hbm.at[part], out_sems.at[d // 32]))
            done[-1].start()
    for copy in done:
        copy.wait()


def surface_blocks(send_order, displacement, velocity, centers, surface_nodes):
    hbm = pl.BlockSpec(memory_space=pltpu.HBM)
    return pl.pallas_call(
        gather_kernel,
        out_shape=jax.ShapeDtypeStruct((SLOTS * 6, BLK), F32),
        in_specs=[hbm] * 5,
        out_specs=hbm,
        scratch_shapes=[
            pltpu.SMEM((1, SLOTS), jnp.int32),
            pltpu.VMEM((3, GRAINS_DEV, NODES), F32),
            pltpu.VMEM((3, GRAINS_DEV, NODES), F32),
            pltpu.VMEM((3, GRAINS_DEV), F32),
            pltpu.VMEM((GRAINS_DEV, SB * BLK), jnp.int32),
            pltpu.VMEM((SLOTS * 8, BLK), F32),
            pltpu.VMEM((SLOTS * 6, BLK), F32),
            pltpu.SemaphoreType.DMA((2,)),
            pltpu.SemaphoreType.DMA((GROUPS, 3)),
            pltpu.SemaphoreType.DMA((GROUPS,)),
        ],
        compiler_params=pltpu.CompilerParams(vmem_limit_bytes=60 * MIB),
        name="surface_blocks",
    )(send_order, displacement, velocity, centers, surface_nodes)


PAIR_UNROLL = 64


def contact_kernel(
    lists_hbm,
    state_ref,
    out_hbm,
    lists_ref,
    left_ref,
    right_ref,
    slide_ref,
    acc_ref,
    out_ref,
    sem,
    out_sems,
):
    fetch = pltpu.make_async_copy(lists_hbm, lists_ref, sem)
    fetch.start()
    scale = math.log2(math.e) / CONTACT_RANGE
    one = jnp.ones((8, BLK), F32)
    pad = jnp.zeros((8, BLK), F32)

    def put(ref, rows, group, values):
        for n, value in enumerate(values):
            ref[pl.ds(pl.multiple_of(group * (rows * 8) + n * 8, 8), 8), :] = value

    def prepare(group, carry):
        first = group * 48
        place = [state_ref[pl.ds(first + c, 8, stride=6), :] - ORIGIN[c] for c in range(3)]
        speed = [state_ref[pl.ds(first + 3 + c, 8, stride=6), :] for c in range(3)]
        norm = place[0] * place[0] + place[1] * place[1] + place[2] * place[2]
        norm = pieces(-scale * norm, 3)
        left, right, slide = [], [], []
        for c in range(3):
            p1, p2, p3 = pieces(place[c], 3)
            q1, q2, q3 = pieces(place[c] * (2.0 * scale), 3)
            left += [p1, p1, p2, p2, p1, p3]
            right += [q1, q2, q1, q2, q3, q1]
        left += norm + [one] * 3
        right += [one] * 3 + norm
        for c in range(3):
            slide += pieces(CONTACT_STIFF * place[c] - CONTACT_DAMP * speed[c], 3)
        slide += [one]
        put(left_ref, 24, group, left)
        put(right_ref, 24, group, right)
        put(slide_ref, 16, group, slide)
        return carry

    lax.fori_loop(0, SLOTS // 8, prepare, 0, unroll=8)
    acc_ref[...] = jnp.zeros_like(acc_ref)
    fetch.wait()
    total = lists_ref[2, 0]

    def rows(ref, count, slot):
        return ref[pl.ds((slot >> 3) * (count * 8) + (slot & 7), count, stride=8), :]

    def batch(first, pairs):
        chosen = []
        for n in range(pairs):
            flat = first + n
            in_range = flat < total
            at = jnp.minimum(flat, SLOTS - 1)
            i = jnp.where(in_range, lists_ref[0, at], 0)
            j = jnp.where(in_range, lists_ref[1, at], 0)
            chosen.append((i, j, jnp.where(in_range, i, SLOTS), jnp.where(in_range, j, SLOTS)))
        weights = []
        for i, j, _, _ in chosen:
            left = jnp.concatenate([rows(left_ref, 24, i), pad], axis=0).astype(BF16)
            right = jnp.concatenate([rows(right_ref, 24, j), pad], axis=0).astype(BF16)
            exponent = lax.dot_general(left, right, ALONG, preferred_element_type=F32)
            weights.append(jnp.exp2(exponent))
        sums = []
        for (i, j, _, _), weight in zip(chosen, weights):
            slide_i = rows(slide_ref, 16, i).astype(BF16)
            slide_j = rows(slide_ref, 16, j).astype(BF16)
            to_i = lax.dot_general(
                jnp.concatenate([slide_j, slide_j], axis=1),
                jnp.concatenate(halves(weight.T), axis=0),
                DOWN,
                preferred_element_type=F32,
            )
            to_j = lax.dot_general(
                jnp.concatenate([slide_i, slide_i], axis=1),
                jnp.concatenate(halves(weight), axis=0),
                DOWN,
                preferred_element_type=F32,
            )
            sums.append((to_i, to_j))
        for (_, _, i, j), (to_i, to_j) in zip(chosen, sums):
            rows_i = pl.ds(pl.multiple_of(i * 16, 16), 16)
            acc_ref[rows_i, :] += to_i
            rows_j = pl.ds(pl.multiple_of(j * 16, 16), 16)
            acc_ref[rows_j, :] += to_j

    def full_batch(step, carry):
        batch(step * PAIR_UNROLL, PAIR_UNROLL)
        return carry

    half = PAIR_UNROLL // 2
    whole = (total + half - 1) // PAIR_UNROLL
    lax.fori_loop(0, whole, full_batch, 0)

    @pl.when(total > whole * PAIR_UNROLL)
    def _():
        batch(whole * PAIR_UNROLL, half)

    def finish(group):
        def acc(n):
            return acc_ref[pl.ds(group * 128 + n, 8, stride=16), :]

        def slide(n):
            return slide_ref[group * 128 + n * 8 : group * 128 + n * 8 + 8, :]

        total_weight = acc(9)
        for c in range(3):
            own = slide(3 * c) + slide(3 * c + 1) + slide(3 * c + 2)
            other = acc(3 * c) + acc(3 * c + 1) + acc(3 * c + 2)
            out_ref[pl.ds(group * 24 + c, 8, stride=3), :] = own * total_weight - other

    done = []
    for group in range(SLOTS // 8):
        finish(group)
        if group % 4 == 3:
            part = pl.ds(24 * (group - 3), 96)
            done.append(pltpu.make_async_copy(out_ref.at[part], out_hbm.at[part], out_sems.at[group // 4]))
            done[-1].start()
    for copy in done:
        copy.wait()


def contact_forces(lists, state):
    vmem = pl.BlockSpec(memory_space=pltpu.VMEM)
    hbm = pl.BlockSpec(memory_space=pltpu.HBM)
    return pl.pallas_call(
        contact_kernel,
        out_shape=jax.ShapeDtypeStruct((SLOTS * 3, BLK), F32),
        in_specs=[pl.BlockSpec(memory_space=pl.ANY), vmem],
        out_specs=hbm,
        scratch_shapes=[
            pltpu.SMEM((8, SLOTS), jnp.int32),
            pltpu.VMEM((SLOTS * 24, BLK), F32),
            pltpu.VMEM((SLOTS * 24, BLK), F32),
            pltpu.VMEM((SLOTS * 16, BLK), F32),
            pltpu.VMEM(((SLOTS + 1) * 16, BLK), F32),
            pltpu.VMEM((SLOTS * 3, BLK), F32),
            pltpu.SemaphoreType.DMA,
            pltpu.SemaphoreType.DMA((4,)),
        ],
        compiler_params=pltpu.CompilerParams(vmem_limit_bytes=24 * MIB),
        name="contact_forces",
    )(lists, state)


TILE_UNROLL = 16
TILES = 4
BOND_PARTS = ((0, 8), (8, 24))


def bond_kernel(
    first_grain,
    grains,
    tiles_ref,
    disp_ref,
    words_ref,
    out_ref,
    base_ref,
    other_ref,
    fixed_ref,
    rest_ref,
    inverse_rest_ref,
    flag_ref,
    dead_ref,
    acc_ref,
    list_ref,
):
    lane = lane_iota((8, BLK))
    sub = sublane_iota((8, BLK))
    one = jnp.ones((8, BLK), F32)
    zero = jnp.zeros((8, BLK), F32)

    def lattice(a, c):
        index = lane + a * BLK
        return ((index & 7, (index >> 3) & 7, index >> 6)[c]).astype(F32) - ORIGIN[c]

    count = jnp.int32(0)
    for grain in range(grains):
        for t in range(TILES):
            apart = tiles_ref[t, 0, first_grain + grain] - tiles_ref[t, 1, first_grain + grain]
            list_ref[count] = grain * TILES + t
            count += jnp.where((apart >= -REACH) & (apart <= REACH), 1, 0)

    for a in range(NB):
        rows = jnp.where(sub < 6, 0.0, 1.0)
        for c in range(3):
            rows = jnp.where((sub == c) | (sub == c + 3), -2.0 * lattice(a, c), rows)
        fixed_ref[a * 8 : a * 8 + 8, :] = rows

    col_y = (lane >> 3) & 7
    for apart in range(-REACH, REACH + 1):
        for r in range(16):
            dx = sub - (lane & 7)
            dy = (r & 7) - col_y
            dz = (r >> 3) - (lane >> 6) - 2 * apart
            square = dx * dx + dy * dy + dz * dz
            near = (square >= 1) & (square <= 9)
            row = ((apart + REACH) * 16 + r) * 8
            rest = square.astype(F32)
            rest_ref[row : row + 8, :] = rest
            inverse_rest_ref[row : row + 8, :] = lax.rsqrt(jnp.maximum(rest, 1.0))
            flag_ref[row : row + 8, :] = jnp.where(near, jnp.left_shift(1, lane & 7), 0)
            dead_ref[row : row + 8, :] = jnp.where(near, 0, 1)

    for group in range(grains // 8):
        these = pl.ds(first_grain + 8 * group, 8)
        for a in range(NB):
            high, low, growth = [], [], None
            for c in range(3):
                u1, u2 = pieces(disp_ref[c, these, a * BLK : (a + 1) * BLK], 2)
                high.append(u1)
                low.append(u2)
                both = u1 + u2
                term = both * (2.0 * lattice(a, c) + both)
                growth = term if growth is None else growth + term
            g1, g2, g3 = pieces(growth, 3)
            minus_high = [-2.0 * v for v in high]
            minus_low = [-2.0 * v for v in low]
            row = (group * NB + a) * 80
            for n, value in enumerate([one, g3] + high + low + [g1, g2]):
                base_ref[row + n * 8 : row + n * 8 + 8, :] = value
            row = (group * NB + a) * 104
            for n, value in enumerate([g3, one] + minus_high + minus_low + minus_high + [zero, zero]):
                other_ref[row + n * 8 : row + n * 8 + 8, :] = value

    acc_ref[...] = jnp.zeros_like(acc_ref)

    tile_row = sublane_iota((BLK, BLK))
    tile_col = lane_iota((BLK, BLK))
    spread = jnp.where((tile_row & 15) == (tile_col >> 3), 1.0, 0.0).astype(BF16)
    own_lane = (lane >> 4) == sub

    def batch(step, carry):
        chosen = []
        for n in range(TILE_UNROLL):
            flat = step * TILE_UNROLL + n
            in_range = flat < count
            tile = list_ref[jnp.where(in_range, flat, 0)]
            grain, t = tile >> 2, tile & 3
            a = tiles_ref[t, 0, first_grain + grain]
            b = tiles_ref[t, 1, first_grain + grain]
            target = jnp.where(in_range, grain * NB + a, grains * NB)
            chosen.append((grain, t, a, b, target))

        def rows(ref, per, grain, a, first):
            start = ((grain >> 3) * NB + a) * (per * 8) + first * 8 + (grain & 7)
            return ref[pl.ds(start, 8, stride=8), :]

        def fixed(a):
            return fixed_ref[pl.ds(pl.multiple_of(a * 8, 8), 8), :]

        growths, words = [], []
        for grain, t, a, b, _ in chosen:
            base_a = rows(base_ref, 10, grain, a, 2)
            left = jnp.concatenate([base_a, fixed(a), rows(base_ref, 10, grain, a, 0), base_a], axis=0)
            right = jnp.concatenate(
                [
                    fixed(b),
                    rows(base_ref, 10, grain, b, 2),
                    rows(other_ref, 13, grain, b, 0),
                    rows(other_ref, 13, grain, b, 5),
                ],
                axis=0,
            ).astype(BF16)
            growths.append(jnp.dot(left.T.astype(BF16), right, preferred_element_type=F32))
            word = words_ref[pl.ds((first_grain + grain) * 64 + t, 16, stride=4), :].astype(F32)
            picked = jnp.concatenate(
                [jnp.where(own_lane, jnp.broadcast_to(word[r : r + 1, :], (8, BLK)), 0.0) for r in range(16)],
                axis=0,
            ).astype(BF16)
            words.append(jnp.dot(picked, spread, preferred_element_type=F32).astype(jnp.int32))
        pulls = []
        for (grain, t, a, b, _), growth, word in zip(chosen, growths, words):
            apart = jnp.clip(b - a, -REACH, REACH) + REACH
            table = pl.ds(pl.multiple_of(apart * BLK, BLK), BLK)
            live = (word & flag_ref[table, :]) == dead_ref[table, :]
            pull = inverse_rest_ref[table, :] - lax.rsqrt(rest_ref[table, :] + growth)
            pulls.append(jnp.where(live, pull, 0.0))
        forces = []
        for (grain, t, a, b, _), pull in zip(chosen, pulls):
            high, low = halves(pull)
            moments = jnp.concatenate([rows(base_ref, 10, grain, b, 2), fixed(b)], axis=0).astype(BF16)
            forces.append(
                lax.dot_general(
                    jnp.concatenate([high, low], axis=1),
                    jnp.concatenate([moments, moments], axis=1),
                    ACROSS,
                    preferred_element_type=F32,
                ).T
            )
        for (_, _, _, _, target), force in zip(chosen, forces):
            acc_ref[pl.ds(pl.multiple_of(target * 16, 16), 16), :] += force
        return carry

    lax.fori_loop(0, (count + TILE_UNROLL - 1) // TILE_UNROLL, batch, 0)

    for group in range(grains // 8):
        for a in range(NB):
            row = (group * 8 * NB + a) * 16
            acc = [acc_ref[pl.ds(row + n, 8, stride=NB * 16), :] for n in (0, 1, 2, 3, 4, 5, 8, 9, 10, 14)]
            base = (group * NB + a) * 80
            for c in range(3):
                own = lattice(a, c) + (
                    base_ref[base + 16 + 8 * c : base + 24 + 8 * c, :]
                    + base_ref[base + 40 + 8 * c : base + 48 + 8 * c, :]
                )
                force = acc[c] + acc[3 + c] - 0.5 * acc[6 + c] - acc[9] * own
                out_ref[c, 8 * group : 8 * group + 8, a * BLK : (a + 1) * BLK] = force * BOND_STIFF


def bond_forces(first_grain, grains, tile_list, displacement, words):
    vmem = pl.BlockSpec(memory_space=pltpu.VMEM)
    smem = pl.BlockSpec(memory_space=pltpu.SMEM)
    blocks = grains * NB
    table = (2 * REACH + 1) * BLK
    return pl.pallas_call(
        functools.partial(bond_kernel, first_grain, grains),
        out_shape=jax.ShapeDtypeStruct((3, grains, NODES), F32),
        in_specs=[smem, vmem, vmem],
        out_specs=vmem,
        scratch_shapes=[
            pltpu.VMEM((blocks * 10, BLK), F32),
            pltpu.VMEM((blocks * 13, BLK), F32),
            pltpu.VMEM((NB * 8, BLK), F32),
            pltpu.VMEM((table, BLK), F32),
            pltpu.VMEM((table, BLK), F32),
            pltpu.VMEM((table, BLK), jnp.int32),
            pltpu.VMEM((table, BLK), jnp.int32),
            pltpu.VMEM(((blocks + 1) * 16, BLK), F32),
            pltpu.SMEM((grains * TILES + 1,), jnp.int32),
        ],
        compiler_params=pltpu.CompilerParams(vmem_limit_bytes=24 * MIB),
        cost_estimate=pl.CostEstimate(flops=2_000_000_000, transcendentals=2_000_000, bytes_accessed=2_000_000),
        name="bond_forces",
    )(tile_list, displacement, words)


def inverse_kernel(count_ref, nodes_ref, pairs_ref, send_ref, out_ref, lists_ref):
    lists_ref[:2, :] = pairs_ref[...]
    lists_ref[2:3, :] = jnp.full((1, SLOTS), count_ref[0], jnp.int32)
    block = send_ref[...]
    grain = block >> 2
    lists_ref[3:4, :] = ((grain >> 3) * SB + (block & 3)) * 24 + (grain & 7)
    lists_ref[4:, :] = jnp.zeros((4, SLOTS), jnp.int32)
    sub128 = sublane_iota((BLK, SB * BLK))
    sub16 = sublane_iota((16, SB * BLK))
    k_index = lane_iota((16, SB * BLK))
    k_value = jnp.where(sub16 < 8, k_index & 127, 1 + (k_index >> 7)).astype(F32)

    def step(part, carry):
        for n in range(8):
            grain = part * 8 + n
            node = nodes_ref[pl.ds(grain, 1), :]
            hit = jnp.where(jnp.broadcast_to(node & 127, (BLK, SB * BLK)) == sub128, 1.0, 0.0).astype(BF16)
            block = jnp.broadcast_to(node >> 7, (16, SB * BLK))
            value = jnp.where(block == (sub16 & 7), k_value, 0.0).astype(BF16)
            out_ref[pl.ds(pl.multiple_of(grain * 16, 16), 16), :] = lax.dot_general(
                value, hit, ACROSS, preferred_element_type=F32
            )
        return carry

    lax.fori_loop(0, GRAINS_DEV // 8, step, 0)


def surface_places(pair_count, surface_nodes, pairs, send_order):
    vmem = pl.BlockSpec(memory_space=pltpu.VMEM)
    return pl.pallas_call(
        inverse_kernel,
        out_shape=(
            jax.ShapeDtypeStruct((GRAINS_DEV * 16, BLK), F32),
            jax.ShapeDtypeStruct((8, SLOTS), jnp.int32),
        ),
        in_specs=[pl.BlockSpec(memory_space=pltpu.SMEM), vmem, vmem, vmem],
        out_specs=(vmem, vmem),
        compiler_params=pltpu.CompilerParams(vmem_limit_bytes=8 * MIB),
        cost_estimate=pl.CostEstimate(flops=500_000_000, transcendentals=0, bytes_accessed=500_000),
        name="surface_places",
    )(pair_count, surface_nodes, pairs, send_order)


def sum_kernel(bonds, lists_hbm, back_ref, inverse_ref, vel_ref, *refs):
    bond_refs = refs[:bonds]
    force_hbm, new_hbm, lists_ref, force_ref, new_ref, block_ref, lists_sem, out_sems = refs[bonds:]
    fetch = pltpu.make_async_copy(lists_hbm, lists_ref, lists_sem)
    fetch.start()
    places = []
    for group in range(GROUPS):
        for a in range(NB):
            lane = inverse_ref[pl.ds(group * 128 + a, 8, stride=16), :].astype(jnp.int32)
            block = inverse_ref[pl.ds(group * 128 + 8 + a, 8, stride=16), :].astype(jnp.int32)
            places.append((lane, block))
    fetch.wait()
    for d in range(SLOTS):
        block_ref[pl.ds(lists_ref[3, d], 3, stride=8), :] = back_ref[3 * d : 3 * d + 3, :]
    done = []
    for group in range(GROUPS):
        grains = pl.ds(8 * group, 8)
        part = max(n for n in range(bonds) if BOND_PARTS[n][0] <= 8 * group)
        bond_ref = bond_refs[part]
        bond_grains = pl.ds(8 * group - BOND_PARTS[part][0], 8)
        for a in range(NB):
            lane, block = places[group * NB + a]
            columns = slice(a * BLK, (a + 1) * BLK)
            for c in range(3):
                value = jnp.zeros((8, BLK), F32)
                for k in range(SB):
                    start = (group * SB + k) * 24 + c * 8
                    value = jnp.where(block == k + 1, lane_gather(block_ref[start : start + 8, :], lane), value)
                force = bond_ref[c, bond_grains, columns] + value
                force_ref[c, grains, columns] = force
                new_ref[c, grains, columns] = vel_ref[c, grains, columns] + TIME_STEP * force
        for n, (source, target) in enumerate(((force_ref, force_hbm), (new_ref, new_hbm))):
            done.append(pltpu.make_async_copy(source.at[:, grains], target.at[:, grains], out_sems.at[group, n]))
            done[-1].start()
    for copy in done:
        copy.wait()


def sum_forces(lists, returned, inverse, velocity, bonds):
    vmem = pl.BlockSpec(memory_space=pltpu.VMEM)
    hbm = pl.BlockSpec(memory_space=pltpu.HBM)
    shape = (3, GRAINS_DEV, NODES)
    return pl.pallas_call(
        functools.partial(sum_kernel, len(bonds)),
        out_shape=(jax.ShapeDtypeStruct(shape, F32),) * 2,
        in_specs=[pl.BlockSpec(memory_space=pl.ANY)] + [vmem] * (3 + len(bonds)),
        out_specs=(hbm, hbm),
        scratch_shapes=[
            pltpu.SMEM((8, SLOTS), jnp.int32),
            pltpu.VMEM(shape, F32),
            pltpu.VMEM(shape, F32),
            pltpu.VMEM((SLOTS * 3, BLK), F32),
            pltpu.SemaphoreType.DMA,
            pltpu.SemaphoreType.DMA((GROUPS, 2)),
        ],
        compiler_params=pltpu.CompilerParams(vmem_limit_bytes=8 * MIB),
        name="sum_forces",
    )(lists, returned, inverse, velocity, *bonds)


def exchange(rows, width):
    moved = lax.all_to_all(
        rows.reshape(SLOTS, 1, width, BLK), ("grain", "cell"), split_axis=0, concat_axis=0, tiled=True
    )
    return moved.reshape(SLOTS * width, BLK)


def on_device(
    displacement,
    velocity,
    centers,
    tile_list,
    broken_bits,
    surface_nodes,
    send_order,
    pair_list,
    pair_count,
):
    displacement = displacement.transpose(1, 0, 2)
    velocity = velocity.transpose(1, 0, 2)
    tiles = tile_list.transpose(1, 2, 0)
    words = broken_bits.reshape(GRAINS_DEV, TILES, 16, BLK).transpose(0, 2, 1, 3).reshape(GRAINS_DEV * 64, BLK)
    outgoing = surface_blocks(send_order, displacement, velocity, centers, surface_nodes)
    received = exchange(outgoing, 6)
    inverse, lists = surface_places(pair_count, surface_nodes, pair_list[0].T, send_order)
    bonds = [bond_forces(first, count, tiles, displacement, words) for first, count in BOND_PARTS]
    received, lists, bonds[0] = lax.optimization_barrier((received, lists, bonds[0]))
    slot_force = contact_forces(lists, received)
    returned = exchange(slot_force, 3)
    force, new_velocity = sum_forces(lists, returned, inverse, velocity, bonds)
    return force.transpose(1, 0, 2), new_velocity.transpose(1, 0, 2)


def solution(mesh):
    return jax.shard_map(
        on_device,
        mesh=mesh,
        in_specs=(
            P(("grain", "cell"), None, None),
            P(("grain", "cell"), None, None),
            P(None, ("grain", "cell")),
            P(("grain", "cell"), None, None),
            P(("grain", "cell"), None, None),
            P(("grain", "cell"), None),
            P(("grain", "cell"), None),
            P(("grain", "cell"), None, None),
            P(("grain", "cell")),
        ),
        out_specs=(P(("grain", "cell"), None, None), P(("grain", "cell"), None, None)),
        check_vma=False,
    )
```
